128 devices in a mesh: blk: 32 (over x_hi, z, y), grp: 4 (over x_lo, core).
Axes of the slice: x: 4 (x_hi: 2, x_lo: 2; x = x_hi * 2 + x_lo), y: 4, z: 4, core: 2. Of those that a mesh axis runs over, the one named last changes fastest.
Arguments:
- images: bfloat16 [8192, 1536], P('blk'), may hold values from -100 to 100
- defocus: float32 [8192], P('blk'), may hold values from 1 to 12
- class_id: int32 [8192, 1], P('blk'), may hold values from 0 to 255; in each aligned block of 256 rows (0 to 255, 256 to 511, ...) at most 2 rows name the same one
- rotation_id: int32 [8192], P('blk'), may hold values from 0 to 31
- shift_id: int32 [8192], P('blk'), may hold values from 0 to 8
- references: float32 [4, 64, 1536], P('grp', 'blk'), may hold values from -4 to 4
- owner: int32 [4, 64], P('grp'), may hold values from 0 to 63, as said below
- inv_noise: float32 [24], replicated, may hold values from 0.5 to 2
- prior: float32 [24], replicated, may hold values from 0.5 to 2
Outputs:
- evidence: float32 [8192], P('blk')
- new_refs: float32 [4, 64, 1536], P('grp', 'blk')
The draws below stay inside these ranges and needn't reach their ends.
Inputs may be any that keep to these rules, and one draw needn't show every extreme that they name: `class_id`: among the particles of one index of blk, no class is assigned to more than 2 particles, and some class to exactly 2. `owner`: each row is a permutation of 0 to 63.
All inputs are finite; a program needn't handle non-finite values.
Results may differ from the reference program's by a relative error of at most 0.0036.
Values sent between devices are 32-bit elements; how exact they have to be, the bound alone decides.
No kernel may reach another device: no remote copies, remote signals or barrier semaphores. Data moves between devices by JAX's collectives and lax.ppermute only.
A program may use at most 64 MiB of HBM per device.

```python
import math
import jax
import jax.numpy as jnp
import numpy as np
from jax import lax

CYCLES = 24
ANGLES = 32
SHIFTS = 9
CL_DEV = 2
P_BLK = 256
FEAT = 1536
C_GRP = 64
GROUPS = 4
CLASSES = 256
PARTICLES = 8192
MOST = 2


def draw_owner(key, part):
    row_keys = jax.random.split(key, GROUPS)

    def one_row(row_key):
        return jax.random.permutation(row_key, C_GRP)
    return jax.vmap(one_row)(row_keys).astype(jnp.int32)


def rough_values(key, shape):
    return jnp.clip(jax.random.normal(key, shape, jnp.float32), -4.0, 4.0)


def place_template(pattern, turned, moved):
    angular = jnp.arange(ANGLES, dtype=jnp.int32)
    source = (angular[None, :] - turned[:, None]) % ANGLES
    rotated = jnp.take_along_axis(pattern, jnp.broadcast_to(source[:, None, None, :], pattern.shape), axis=3)
    radius = (jnp.arange(CYCLES, dtype=jnp.float32) + 1.0) / (2.0 * CYCLES)
    bearing = 2.0 * math.pi / ANGLES * jnp.arange(ANGLES, dtype=jnp.float32)
    shift_x = (moved // 3 - 1).astype(jnp.float32)
    shift_y = (moved % 3 - 1).astype(jnp.float32)
    along = shift_x[:, None] * jnp.cos(bearing)[None, :] + shift_y[:, None] * jnp.sin(bearing)[None, :]
    phase = -2.0 * math.pi * radius[None, :, None] * along[:, None, :]
    phase_cos = jnp.cos(phase)
    phase_sin = jnp.sin(phase)
    real_part = phase_cos * rotated[:, 0] - phase_sin * rotated[:, 1]
    imag_part = phase_sin * rotated[:, 0] + phase_cos * rotated[:, 1]
    return jnp.stack([real_part, imag_part], axis=1)


def shared_fields(key):
    focus_key = jax.random.fold_in(key, 101)
    class_key = jax.random.fold_in(key, 102)
    noise_key = jax.random.fold_in(key, 103)
    choice_key = jax.random.fold_in(key, 104)
    faint_key = jax.random.fold_in(key, 105)
    defocus = jnp.exp(jax.random.uniform(focus_key, (PARTICLES,), jnp.float32, 0.0, math.log(12.0)))
    defocus = jnp.clip(defocus, 1.0, 12.0)
    references = rough_values(class_key, (GROUPS, C_GRP, FEAT))
    noise = rough_values(noise_key, (PARTICLES, FEAT))
    sample_keys = jax.random.split(choice_key, 8)
    chosen = jax.random.randint(sample_keys[0], (PARTICLES,), 0, 8) == 0
    picked_class = jax.random.randint(sample_keys[1], (PARTICLES,), 0, CLASSES)
    first_turn = jax.random.randint(sample_keys[2], (PARTICLES,), 0, ANGLES)
    second_turn = (first_turn + jax.random.randint(sample_keys[3], (PARTICLES,), 1, ANGLES)) % ANGLES
    first_move = jax.random.randint(sample_keys[4], (PARTICLES,), 0, SHIFTS)
    second_move = jax.random.randint(sample_keys[5], (PARTICLES,), 0, SHIFTS)
    boost = max(1.0, 40.0 / math.sqrt(FEAT))
    bright = boost * jax.random.uniform(sample_keys[6], (PARTICLES,), jnp.float32, 3.0, 12.0)
    faint = boost * jax.random.uniform(faint_key, (PARTICLES,), jnp.float32, 0.3, 0.6)
    strength = jnp.where(chosen, bright, faint)
    second_strength = strength - boost * jax.random.uniform(sample_keys[7], (PARTICLES,), jnp.float32, 0.08, 0.15)
    frequency = (jnp.arange(CYCLES, dtype=jnp.float32) + 1.0) / CYCLES
    contrast = -jnp.sin(defocus[:, None] * (frequency * frequency)[None, :] + 0.15)
    pattern = references.reshape(CLASSES, 2, CYCLES, ANGLES)[picked_class]
    first_view = place_template(pattern, first_turn, first_move)
    second_view = place_template(pattern, second_turn, second_move)
    signal = strength[:, None, None, None] * first_view + second_strength[:, None, None, None] * second_view
    signal = signal * contrast[:, None, :, None]
    images = jnp.clip(noise + signal.reshape(PARTICLES, FEAT), -100.0, 100.0)
    return (defocus, references, images)


def draw_defocus(key, part):
    return shared_fields(key)[0].astype(jnp.float32)


def draw_references(key, part):
    return shared_fields(key)[1].astype(jnp.float32)


def draw_images(key, part):
    return shared_fields(key)[2].astype(jnp.bfloat16)


def touch_ends(values, rng, least, largest):
    index_at = [jax.random.randint(jax.random.fold_in(rng, axis), (), 0, length) for axis, length in enumerate(values.shape)]
    longest = values.shape.index(max(values.shape))
    beside = index_at[:longest] + [(index_at[longest] + 1) % values.shape[longest]] + index_at[longest + 1:]
    return values.at[tuple(index_at)].set(least).at[tuple(beside)].set(largest)


def routed_block(key, own, number, rows, amount, top, most, lean):
    ranking = jax.random.permutation(key, amount)
    heavy_load, usual = load_shares(amount, rows * top, most, lean, True), load_shares(amount, rows * top, most, lean, False)
    places = jnp.arange(amount)

    def named(sizes, rotation):
        used = int((sizes > 0).sum())
        fixed = max(1, used // 4)
        shifted = fixed + (places - fixed + rotation * (used - fixed)) % max(1, amount - fixed)
        return jnp.zeros((amount,), jnp.int32).at[ranking[jnp.where(places < fixed, places, shifted)]].set(jnp.asarray(sizes, jnp.int32))

    sizes = jnp.where(number % 4 == 0, named(heavy_load, number // 4), named(usual, number - number // 4 - 1))
    mixed = jax.random.permutation(jax.random.fold_in(own, 3), amount)
    source_of, sink = mixed[0:amount // 2 * 2:2], mixed[1:amount // 2 * 2:2]
    room = jnp.minimum(sizes[source_of] - 1, most - sizes[sink]) // 2
    room = jnp.where((source_of == ranking[0]) | (sink == ranking[0]) | (sizes[sink] == 0), 0, jnp.maximum(room, 0))
    shifted = jax.random.randint(jax.random.fold_in(own, 4), (amount // 2,), 0, 1 << 20) % (room + 1)
    sizes = sizes.at[source_of].add(-shifted).at[sink].add(shifted)
    members = jnp.searchsorted(jnp.cumsum(sizes), jnp.arange(rows * top), side="right").astype(jnp.int32)
    listing = members.reshape(top, rows).T
    listing = listing[jax.random.permutation(jax.random.fold_in(own, 1), rows)]
    rotation = jax.random.randint(jax.random.fold_in(own, 2), (rows, 1), 0, top)
    return jnp.take_along_axis(listing, (jnp.arange(top)[None, :] + rotation) % top, axis=1)


def load_shares(amount, total, most, lean, full):
    weights = [(1 << 20) // math.isqrt(rank ** lean) + 1 for rank in range(1, amount + 1)]
    largest = most if full else min(most, max(-(-total // amount), total * weights[0] // sum(weights)))
    least = 1 if total - largest >= amount - 1 else 0
    holding, surplus = [largest] + [least] * (amount - 1), total - largest - least * (amount - 1)
    while surplus > 0:
        free = [i for i in range(1, amount) if holding[i] < largest] or [i for i in range(1, amount) if holding[i] < most]
        whole, budget = sum([weights[i] for i in free]), surplus
        for i in free:
            extra = min(most - holding[i], max(1, budget * weights[i] // whole), surplus)
            holding[i] = holding[i] + extra
            surplus = surplus - extra
    return np.array(holding)


def setup_inputs(seed: int = 0) -> dict:
    splits = jax.random.split(jax.random.key(seed), 10)
    images = draw_images(jax.random.fold_in(splits[9], 71), 0)
    defocus = draw_defocus(jax.random.fold_in(splits[9], 71), 0)
    class_id_keys = jax.random.split(jax.random.fold_in(splits[2], 1), PARTICLES // P_BLK)
    class_id_turns = jax.random.permutation(jax.random.fold_in(splits[2], 3), PARTICLES // P_BLK)
    class_id = jax.vmap(lambda own, number: routed_block(jax.random.fold_in(splits[2], 2), own, number, P_BLK, CLASSES, 1, MOST, 3))(class_id_keys, class_id_turns).reshape((PARTICLES, 1))
    rotation_id = touch_ends(jax.random.randint(splits[3], (PARTICLES,), 0, ANGLES), jax.random.fold_in(splits[3], 1), 0, ANGLES - 1).astype(jnp.int32)
    shift_id = touch_ends(jax.random.randint(splits[4], (PARTICLES,), 0, SHIFTS), jax.random.fold_in(splits[4], 1), 0, SHIFTS - 1).astype(jnp.int32)
    references = draw_references(jax.random.fold_in(splits[9], 71), 0)
    owner = draw_owner(jax.random.fold_in(splits[9], 71), 0)
    inv_noise = jnp.clip(jnp.exp(jax.random.uniform(splits[7], (CYCLES,), jnp.float32, math.log(0.5), math.log(2.0))), 0.5, 2.0)
    prior = jnp.clip(jnp.exp(jax.random.uniform(splits[8], (CYCLES,), jnp.float32, math.log(0.5), math.log(2.0))), 0.5, 2.0)
    return {"images": images, "defocus": defocus, "class_id": class_id, "rotation_id": rotation_id, "shift_id": shift_id, "references": references, "owner": owner, "inv_noise": inv_noise, "prior": prior}


def contrast_table(defocus):
    frequency = (jnp.arange(CYCLES, dtype=jnp.float32) + 1.0) / CYCLES
    return -jnp.sin(defocus[:, None] * (frequency * frequency)[None, :] + 0.15)

def phase_tables():
    radius = (jnp.arange(CYCLES, dtype=jnp.float32) + 1.0) / (2.0 * CYCLES)
    bearing = 2.0 * math.pi / ANGLES * jnp.arange(ANGLES, dtype=jnp.float32)
    shift_index = jnp.arange(SHIFTS, dtype=jnp.int32)
    shift_x = (shift_index // 3 - 1).astype(jnp.float32)
    shift_y = (shift_index % 3 - 1).astype(jnp.float32)
    along = shift_x[:, None] * jnp.cos(bearing)[None, :] + shift_y[:, None] * jnp.sin(bearing)[None, :]
    phase = -2.0 * math.pi * radius[None, :, None] * along[:, None, :]
    return (jnp.cos(phase), jnp.sin(phase))

def weigh(images, factor):
    row_total = images.shape[0]
    grid = images.astype(jnp.float32).reshape(row_total, 2, CYCLES, ANGLES)
    return (grid * factor[:, None, :, None]).reshape(row_total, -1).astype(jnp.bfloat16)

def make_templates(ref_block):
    block_rows = ref_block.shape[0]
    grid = ref_block.reshape(block_rows, 2, CYCLES, ANGLES)
    angular = jnp.arange(ANGLES, dtype=jnp.int32)
    turning = (angular[:, None, None] == (angular[None, None, :] - angular[None, :, None]) % ANGLES).astype(jnp.float32)
    rotated = jnp.einsum('nqka,arb->nrqkb', grid, turning, precision=lax.Precision.HIGHEST)
    phase_cos, phase_sin = phase_tables()
    rotated_re = rotated[:, :, 0][:, :, None]
    rotated_im = rotated[:, :, 1][:, :, None]
    real_part = phase_cos[None, None] * rotated_re - phase_sin[None, None] * rotated_im
    imag_part = phase_sin[None, None] * rotated_re + phase_cos[None, None] * rotated_im
    stacked = jnp.stack([real_part, imag_part], axis=3)
    return stacked.reshape(block_rows * ANGLES * SHIFTS, -1).astype(jnp.bfloat16)

def score_block(ref_block, weighted, contrast_power, score_scale):
    block_rows = ref_block.shape[0]
    templates = make_templates(ref_block)
    cross = lax.dot_general(templates, weighted, (((1,), (1,)), ((), ())), preferred_element_type=jnp.float32)
    grid = ref_block.reshape(block_rows, 2, CYCLES, ANGLES)
    power = lax.optimization_barrier(jnp.sum(grid * grid, axis=(1, 3)))
    penalty = jnp.dot(power, contrast_power.T, precision=lax.Precision.HIGHEST)
    logits = (cross.reshape(block_rows, ANGLES * SHIFTS, -1) - 0.5 * penalty[:, None, :]) * score_scale
    return logits.reshape(block_rows * ANGLES * SHIFTS, -1)

def target_rows(relative, rotation_id, shift_id):
    inside = (relative >= 0) & (relative < CL_DEV)
    return jnp.where(inside, (relative * ANGLES + rotation_id) * SHIFTS + shift_id, -1).astype(jnp.int32)

def update(running, logits, target):
    peak, total, picked = running
    new_peak = jnp.maximum(peak, lax.optimization_barrier(jnp.max(logits, axis=0)))
    total = total * jnp.exp(peak - new_peak) + lax.optimization_barrier(jnp.sum(jnp.exp(logits - new_peak[None, :]), axis=0))
    row_index = jnp.arange(logits.shape[0], dtype=jnp.int32)
    picked = picked + lax.optimization_barrier(jnp.sum(jnp.where(row_index[:, None] == target[None, :], logits, 0.0), axis=0))
    return (new_peak, total, picked)

def align_terms(images, contrast, weight, rotation_id, shift_id):
    row_total = images.shape[0]
    phase_cos, phase_sin = phase_tables()
    chosen = (shift_id[:, None] == jnp.arange(SHIFTS, dtype=jnp.int32)[None, :]).astype(jnp.float32)
    cos_rows = jnp.dot(chosen, phase_cos.reshape(SHIFTS, -1), precision=lax.Precision.HIGHEST).reshape(row_total, CYCLES, ANGLES)
    sin_rows = jnp.dot(chosen, phase_sin.reshape(SHIFTS, -1), precision=lax.Precision.HIGHEST).reshape(row_total, CYCLES, ANGLES)
    grid = images.astype(jnp.float32).reshape(row_total, 2, CYCLES, ANGLES)
    unshift_re = cos_rows * grid[:, 0] + sin_rows * grid[:, 1]
    unshift_im = cos_rows * grid[:, 1] - sin_rows * grid[:, 0]
    unshifted = jnp.stack([unshift_re, unshift_im], axis=1)
    angular = jnp.arange(ANGLES, dtype=jnp.int32)
    turning = (angular[None, :, None] == (angular[None, None, :] + rotation_id[:, None, None]) % ANGLES).astype(jnp.float32)
    aligned = jnp.einsum('pqka,pab->pqkb', unshifted, turning, precision=lax.Precision.HIGHEST)
    scaled = weight[:, None] * contrast
    numer_term = (aligned * scaled[:, None, :, None]).reshape(row_total, -1)
    denom_term = weight[:, None] * contrast * contrast
    return (numer_term, denom_term)

def finish(numerator, denominator, prior):
    grid = numerator.reshape(-1, 2, CYCLES, ANGLES)
    return (grid / (denominator + prior[None, :])[:, None, :, None]).reshape(numerator.shape)

def reference(images, defocus, class_id, rotation_id, shift_id, references, owner, inv_noise, prior):
    contrast = contrast_table(defocus)
    contrast_power = contrast * contrast * inv_noise[None, :]
    weighted = weigh(images, contrast * inv_noise[None, :])
    score_scale = 1.0 / math.sqrt(FEAT)
    labels = class_id[:, 0]
    blocks = references.reshape(CLASSES // CL_DEV, CL_DEV, FEAT)
    firsts = CL_DEV * jnp.arange(CLASSES // CL_DEV, dtype=jnp.int32)

    def visit(running, entries):
        ref_block, block_first = entries
        logits = score_block(ref_block, weighted, contrast_power, score_scale)
        return (update(running, logits, target_rows(labels - block_first, rotation_id, shift_id)), None)
    initial = (jnp.full((PARTICLES,), -1e+30, jnp.float32), jnp.zeros((PARTICLES,), jnp.float32), jnp.zeros((PARTICLES,), jnp.float32))
    (peak, total, picked), unused = lax.scan(visit, initial, (blocks, firsts))
    log_orients = math.log(CLASSES * ANGLES * SHIFTS)
    log_sum = peak + jnp.log(total)
    evidence = log_sum - log_orients
    weight = jnp.exp(picked - log_sum + log_orients)
    numer_term, denom_term = align_terms(images, contrast, weight, rotation_id, shift_id)
    slots = (labels // C_GRP * C_GRP + owner.reshape(-1)[labels]).astype(jnp.int32)
    numerator = jax.ops.segment_sum(numer_term, slots, num_segments=CLASSES)
    denominator = jax.ops.segment_sum(denom_term, slots, num_segments=CLASSES)
    new_refs = finish(numerator, denominator, prior).reshape(GROUPS, C_GRP, FEAT)
    return (evidence, new_refs)
```

```python
import functools
import math

import jax
import jax.numpy as jnp
import numpy as np
from jax import lax
from jax.experimental import pallas as pl
from jax.experimental.pallas import tpu as pltpu
from jax.sharding import PartitionSpec as P

CYCLES = 24
ANGLES = 32
SHIFTS = 9
CL_DEV = 2
P_BLK = 256
FEAT = 1536
HALF = FEAT // 2
C_GRP = 64
GROUPS = 4
CLASSES = 256
BLKS = 32
ROWS = 2 * C_GRP
PAIRS = 8
KGRP = 6
WIDE = FEAT + 128
LOG_ORIENTS = math.log(CLASSES * ANGLES * SHIFTS)
HIGH = lax.Precision.HIGHEST
F32 = jnp.float32
BF16 = jnp.bfloat16


def slot_place(s):
    if s == 0:
        return PAIRS - 1, 0
    if s == 8:
        return PAIRS - 1, 1
    return (s - 1, 0) if s < 8 else (15 - s, 1)


def phase_np():
    radius = (np.arange(CYCLES) + 1.0) / (2.0 * CYCLES)
    bearing = 2.0 * np.pi / ANGLES * np.arange(ANGLES)
    index = np.arange(SHIFTS)
    dx, dy = index // 3 - 1.0, index % 3 - 1.0
    along = dx[:, None] * np.cos(bearing) + dy[:, None] * np.sin(bearing)
    return -2.0 * np.pi * radius[None, :, None] * along[:, None, :]


def dft_rows():
    theta = 2.0 * np.pi / ANGLES
    angle = np.arange(ANGLES)
    out = np.zeros((16, 2, ANGLES))
    for s in range(1, 16):
        out[s, 0] = np.cos(theta * s * angle)
        out[s, 1] = -np.sin(theta * s * angle)
    out[0, 0] = 1.0
    out[0, 1] = np.cos(np.pi * angle)
    return out


def dft_plain():
    base = dft_rows()
    out = np.zeros((16, 2, 2, 4, 2, 4, ANGLES))
    for q in range(2):
        for k in range(4):
            out[:, :, q, k, q, k, :] = base
    return out.reshape(256, 256)


def turn_table():
    phase = phase_np().reshape(SHIFTS, HALF)
    px, py = phase[7], phase[5]
    columns = [np.cos(px), np.sin(px), np.cos(py), np.sin(py)]
    return np.stack(columns + columns, axis=1).astype(np.float32)


def split(x):
    high = x.astype(np.float32).astype(jnp.bfloat16)
    low = (x - high.astype(np.float64)).astype(np.float32).astype(jnp.bfloat16)
    return high, low


def iota(shape, axis):
    return lax.broadcasted_iota(jnp.int32, shape, axis)


def as_column(row, n):
    same = iota((n, n), 0) == iota((n, n), 1)
    zero = jnp.zeros((), row.dtype)
    return jnp.sum(jnp.where(same, jnp.broadcast_to(row, (n, n)), zero), axis=1, keepdims=True)


def spread_cycles(row):
    column = as_column(row, CYCLES)
    hit = iota((CYCLES, HALF), 0) == iota((CYCLES, HALF), 1) // ANGLES
    return jnp.sum(jnp.where(hit, column, 0.0), axis=0, keepdims=True)


def rows_setup(group, defocus, cls, rot, shf, owner, crow_ref, key_ref, column_ref, turn_ref):
    local = cls - group * C_GRP
    member = (local >= 0) & (local < C_GRP)
    cls_col = as_column(cls, P_BLK)
    earlier = (cls_col == cls) & (iota((P_BLK, P_BLK), 0) < iota((P_BLK, P_BLK), 1))
    turn = jnp.sum(jnp.where(earlier, 1, 0), axis=0, keepdims=True)
    owner_col = as_column(owner, C_GRP)
    hit = iota((C_GRP, P_BLK), 0) == local
    slot = jnp.sum(jnp.where(hit, owner_col, 0), axis=0, keepdims=True)
    key = jnp.where(member, turn * C_GRP + slot, -1)
    key_ref[...] = key
    chosen = iota((ROWS, P_BLK), 0) == key
    pick = lambda row: jnp.sum(jnp.where(chosen, row, jnp.zeros((), row.dtype)), axis=1, keepdims=True)
    focus = jnp.broadcast_to(pick(defocus), (ROWS, 128))
    column_ref[...] = focus
    turn_ref[0] = jnp.broadcast_to(pick(rot), (ROWS, 128))
    turn_ref[1] = jnp.broadcast_to(pick(shf), (ROWS, 128))
    frequency = (iota((1, 128), 1).astype(F32) + 1.0) / CYCLES
    inside = iota((ROWS, 128), 1) < CYCLES
    crow_ref[...] = jnp.where(inside, -jnp.sin(focus * jnp.where(frequency <= 1.0, frequency * frequency, 0.0) + 0.15), 0.0)


def rows_part(g, first, second, table_cos, table_sin, y_ref, cexp_ref, key_ref, column_ref, turn_ref):
    chosen = (iota((ROWS, P_BLK), 0) == key_ref[...]).astype(BF16)
    real = jnp.dot(chosen, first, preferred_element_type=F32)
    imag = jnp.dot(chosen, second, preferred_element_type=F32)
    frequency = ((iota((1, 128), 1) // ANGLES + 4 * g).astype(F32) + 1.0) / CYCLES
    cexp = -jnp.sin(column_ref[...] * (frequency * frequency) + 0.15)
    cexp_ref[...] = cexp
    which = (iota((ROWS, 16), 1) == turn_ref[1][:, :16]).astype(F32)
    cos = jnp.dot(which, table_cos, precision=HIGH, preferred_element_type=F32)
    sin = jnp.dot(which, table_sin, precision=HIGH, preferred_element_type=F32)
    angle = iota((ROWS, 128), 1) % ANGLES
    parts = [cos * real + sin * imag, cos * imag - sin * real]
    for bit in range(5):
        step = 1 << bit
        on = (turn_ref[0] // step) % 2 == 1
        near = angle < ANGLES - step
        for q in range(2):
            x = parts[q]
            moved = jnp.where(near, pltpu.roll(x, 128 - step, 1), pltpu.roll(x, ANGLES - step, 1))
            parts[q] = jnp.where(on, moved, x)
    for q in range(2):
        y_ref[q] = parts[q] * cexp


def prep_kernel(
    group_ref,
    first_ref,
    second_ref,
    defocus_ref,
    cls_ref,
    rot_ref,
    shf_ref,
    owner_ref,
    inv_ref,
    cos_ref,
    sin_ref,
    turns_ref,
    plain_ref,
    what_ref,
    y_ref,
    crow_ref,
    cexp_ref,
    key_ref,
    cp_ref,
    column_ref,
    turn_ref,
    factor_ref,
):
    g = pl.program_id(0)

    @pl.when(g == 0)
    def _():
        defocus = defocus_ref[...]
        frequency = (iota((CYCLES, 1), 0).astype(F32) + 1.0) / CYCLES
        contrast = -jnp.sin((frequency * frequency) * defocus + 0.15)
        inv = as_column(inv_ref[...], CYCLES)
        factor = contrast * inv
        for j in range(KGRP):
            factor_ref[j, 0:4, :] = factor[4 * j : 4 * j + 4]
        cp_ref[...] = jnp.concatenate([contrast * factor, jnp.zeros((128 - CYCLES, P_BLK), F32)], axis=0)
        rows_setup(
            group_ref[0, 0],
            defocus,
            cls_ref[...],
            rot_ref[...],
            shf_ref[...],
            owner_ref[...],
            crow_ref,
            key_ref,
            column_ref,
            turn_ref,
        )

    wide = jnp.concatenate([jnp.broadcast_to(factor_ref[g, k : k + 1, :], (ANGLES, P_BLK)) for k in range(4)], axis=0)
    w0 = first_ref[...].astype(F32).T * wide
    w1 = second_ref[...].astype(F32).T * wide
    tables = [jnp.broadcast_to(turns_ref[:, j : j + 1], (128, P_BLK)) for j in range(4)]

    def moves(v0, v1, c, s):
        c0, c1, s0, s1 = c * v0, c * v1, s * v0, s * v1
        return [(c0 - s1, c1 + s0), (v0, v1), (c0 + s1, c1 - s0)]

    for i, (a0, a1) in enumerate(moves(w0, w1, tables[0], tables[1])):
        for j, (b0, b1) in enumerate(moves(a0, a1, tables[2], tables[3])):
            x = jnp.concatenate([b0, b1], axis=0).astype(BF16)
            res = jnp.dot(plain_ref[...], x, preferred_element_type=F32)
            res = (res[:256] + res[256:]).astype(BF16)
            for s in range(16):
                pair, side = slot_place(s)
                what_ref[3 * i + j, pair, 0, side] = res[16 * s : 16 * s + 16]
    rows_part(
        g, first_ref[...], second_ref[...], cos_ref[...], sin_ref[...], y_ref, cexp_ref, key_ref, column_ref, turn_ref
    )


def real_idft4(e0, e2, re, im):
    a, b = e0 + e2, e0 - e2
    return [a + re, b + im, a - re, b - im]


def real_idft8(c0, c4, c1, c2, c3):
    r = math.sqrt(0.5)
    even = real_idft4(c0 + c4, c2[0], c1[0] + c3[0], c1[1] - c3[1])
    hr, hi = c1[0] - c3[0], c1[1] + c3[1]
    odd = real_idft4(c0 - c4, c2[1], (hr + hi) * r, (hi - hr) * r)
    return even + odd


def real_idft16(a0, a8, a):
    plus = {m: (a[m][0] + a[8 - m][0], a[m][1] - a[8 - m][1]) for m in (1, 2, 3)}
    even = real_idft8(a0 + a8, a[4][0], plus[1], plus[2], plus[3])
    turned = {}
    for m in (1, 2, 3):
        hr, hi = a[m][0] - a[8 - m][0], a[m][1] + a[8 - m][1]
        if m == 2:
            r = math.sqrt(0.5)
            turned[m] = ((hr + hi) * r, (hi - hr) * r)
        else:
            c, s = math.cos(2.0 * math.pi * m / 16), math.sin(2.0 * math.pi * m / 16)
            turned[m] = (hr * c + hi * s, hi * c - hr * s)
    odd = real_idft8(a0 - a8, a[4][1], turned[1], turned[2], turned[3])
    return even + odd


def fold(values, op):
    while len(values) > 1:
        values = [op(values[i], values[i + 1]) if i + 1 < len(values) else values[i] for i in range(0, len(values), 2)]
    return values[0]


def factors(refs_ref, d_high, d_low, lhs_ref):
    scale = math.log2(math.e) / (ANGLES * math.sqrt(FEAT))
    pieces = []
    for h in range(3):
        halves = []
        for q in range(2):
            at = q * HALF + 256 * h
            both = jnp.concatenate([refs_ref[:, at : at + 128], refs_ref[:, at + 128 : at + 256]], axis=0)
            halves.append(both.T)
        pieces.append(jnp.concatenate(halves, axis=0))
    x = jnp.concatenate(pieces, axis=1)
    xh = x.astype(BF16)
    xl = (x - xh.astype(F32)).astype(BF16)
    res = jnp.dot(d_high, xh, preferred_element_type=F32)
    res = res + (jnp.dot(d_low, xh, preferred_element_type=F32) + jnp.dot(d_high, xl, preferred_element_type=F32))
    res = res * scale
    left = iota((8, 128), 1) < 64
    for pair in range(PAIRS):
        slots = (pair + 1, 15 - pair) if pair < PAIRS - 1 else (0, 8)
        blocks = [[[None] * 4 for _ in range(KGRP)] for _ in range(2)]
        for h in range(3):
            lanes = slice(128 * h, 128 * (h + 1))
            v = [(res[16 * s : 16 * s + 8, lanes], res[16 * s + 8 : 16 * s + 16, lanes]) for s in slots]
            outs = []
            if pair < PAIRS - 1:
                m = pair + 1
                c, s = 2.0 * math.cos(2.0 * math.pi * m / ANGLES), 2.0 * math.sin(2.0 * math.pi * m / ANGLES)
                (r0, i0), (r1, i1) = v
                outs.append(((2.0 * r0, 2.0 * i0), (2.0 * r1, 2.0 * i1)))
                outs.append(((2.0 * i0, -2.0 * r0), (-2.0 * i1, 2.0 * r1)))
                outs.append(((c * r0 + s * i0, c * i0 - s * r0), (s * i1 - c * r1, -c * i1 - s * r1)))
                outs.append(((c * i0 - s * r0, -c * r0 - s * i0), (c * i1 + s * r1, s * i1 - c * r1)))
            else:
                (r0, i0), (r1, i1) = v
                zero = jnp.zeros_like(r0)
                outs.append(((r0, i0), (zero, zero)))
                outs.append(((zero, zero), (2.0 * r1, 2.0 * i1)))
                outs.append(((r0, -i0), (zero, zero)))
                outs.append(((zero, zero), (2.0 * i1, -2.0 * r1)))
            for side in range(2):
                for part in range(2):
                    tiles = [o[side][part] for o in outs]
                    for two in range(2):
                        first, second = tiles[2 * two], tiles[2 * two + 1]
                        lower = jnp.where(left, first, pltpu.roll(second, 64, 1))
                        upper = jnp.where(left, pltpu.roll(first, 64, 1), second)
                        blocks[side][2 * h][2 * two + part] = lower
                        blocks[side][2 * h + 1][2 * two + part] = upper
        for two in range(2):
            tall = jnp.concatenate(
                [blocks[side][g][2 * two + part] for g in range(KGRP) for side in range(2) for part in range(2)], axis=0
            )
            lhs_ref[pair, 128 * two : 128 * (two + 1), :] = tall.T.astype(BF16)


def main_kernel(
    refs_ref, what_ref, plain_ref, cp_ref, inv_ref, y_ref, cexp_ref, owner_ref, lse_ref, picked_ref,
    lhs_ref, pen_ref, coef_ref, peak_ref, total_ref
):
    step = pl.program_id(0)
    root = 1.0 / math.sqrt(FEAT)

    @pl.when(step == 0)
    def _():
        factors(refs_ref, plain_ref[:256], plain_ref[256:], lhs_ref)
        refs = refs_ref[...]
        cycle = (iota((FEAT, 128), 0) // ANGLES) % CYCLES
        summing = (cycle == iota((FEAT, 128), 1)).astype(F32)
        power = jnp.dot(refs * refs, summing, precision=HIGH, preferred_element_type=F32)
        penalty = jnp.dot(power, cp_ref[...], precision=HIGH, preferred_element_type=F32)
        pen_ref[...] = penalty * (0.5 * root * math.log2(math.e))
        peak_ref[...] = jnp.full((8, P_BLK), -1e30, F32)
        total_ref[...] = jnp.zeros((8, P_BLK), F32)
        place = (jnp.broadcast_to(owner_ref[...], (C_GRP, C_GRP)) == iota((C_GRP, C_GRP), 0)).astype(F32)
        placed = jnp.dot(place, refs, precision=HIGH, preferred_element_type=F32)
        inv = spread_cycles(inv_ref[...])
        for o in range(2):
            rows = slice(C_GRP * o, C_GRP * (o + 1))
            cexp = cexp_ref[rows, :]
            amount = jnp.zeros((C_GRP, HALF), F32)
            for q in range(2):
                v = placed[:, HALF * q : HALF * (q + 1)]
                scaled = cexp * v
                amount = amount + (y_ref[q, rows, :] * v - 0.5 * scaled * scaled)
            picked_ref[rows, :] = jnp.broadcast_to(
                jnp.sum(amount * inv, axis=1, keepdims=True) * root, (C_GRP, 128)
            )

    for pair in range(PAIRS):
        coef_ref[pair] = jnp.dot(lhs_ref[pair], what_ref[0, pair].reshape(192, P_BLK), preferred_element_type=F32)
    for half in range(2):
        lanes = slice(128 * half, 128 * (half + 1))
        peak, total = peak_ref[:, lanes], total_ref[:, lanes]
        for cb in range(C_GRP // 8):
            take = lambda pair, o: coef_ref[pair, 64 * o + 8 * cb : 64 * o + 8 * cb + 8, lanes]
            pen = pen_ref[8 * cb : 8 * cb + 8, lanes]
            out = []
            for o in (0, 2):
                a = {m: (take(m - 1, o), take(m - 1, o + 1)) for m in range(1, 8)}
                out += real_idft16(take(7, o) - pen, take(7, o + 1), a)
            fresh = jnp.maximum(peak, fold(out, jnp.maximum))
            total = total * jnp.exp2(peak - fresh) + fold([jnp.exp2(x - fresh) for x in out], jnp.add)
            peak = fresh
        peak_ref[:, lanes] = peak
        total_ref[:, lanes] = total

    @pl.when(step == SHIFTS - 1)
    def _():
        peak, total = peak_ref[...], total_ref[...]
        top = jnp.max(peak, axis=0, keepdims=True)
        amount = jnp.sum(total * jnp.exp2(peak - top), axis=0, keepdims=True)
        lse = top * math.log(2.0) + jnp.log(amount)
        lse_ref[...] = jnp.concatenate([lse[:, :128], lse[:, 128:], jnp.zeros((6, 128), F32)], axis=0)


def weigh_kernel(lse_ref, picked_ref, key_ref, y_ref, crow_ref, out_ref):
    lse = jnp.concatenate([lse_ref[0:1, :], lse_ref[1:2, :]], axis=1)
    chosen = iota((ROWS, P_BLK), 0) == key_ref[...]
    mine = jnp.sum(jnp.where(chosen, lse, 0.0), axis=1, keepdims=True)
    valid = jnp.sum(jnp.where(chosen, 1.0, 0.0), axis=1, keepdims=True) > 0.5
    weight = jnp.where(valid, jnp.exp(jnp.where(valid, picked_ref[:, 0:1] - mine + LOG_ORIENTS, 0.0)), 0.0)
    w0, w1 = weight[:C_GRP], weight[C_GRP:]
    for q in range(2):
        out_ref[:, HALF * q : HALF * (q + 1)] = w0 * y_ref[q, :C_GRP] + w1 * y_ref[q, C_GRP:]
    c0, c1 = crow_ref[:C_GRP], crow_ref[C_GRP:]
    out_ref[:, FEAT:] = w0 * c0 * c0 + w1 * c1 * c1


def finish_kernel(got_ref, prior_ref, out_ref):
    total = fold([got_ref[8 * j : 8 * j + 8, :] for j in range(8)], jnp.add)
    total = total[0:4] + total[4:8]
    total = total[0:2] + total[2:4]
    denom = jnp.concatenate([total[:, FEAT:], jnp.ones((6, 128), F32)], axis=0)
    expand = (iota((128, HALF), 0) == iota((128, HALF), 1) // ANGLES).astype(F32)
    wide = jnp.dot(denom, expand, precision=HIGH, preferred_element_type=F32)[0:2]
    wide = wide + spread_cycles(prior_ref[...])
    out_ref[:, :HALF] = total[:, :HALF] / wide
    out_ref[:, HALF:] = total[:, HALF:FEAT] / wide


def params(mib):
    return pltpu.CompilerParams(vmem_limit_bytes=mib << 20)


def whole(shape):
    return pl.BlockSpec(shape, lambda *_: (0,) * len(shape))


def shape(dims, dtype=F32):
    return jax.ShapeDtypeStruct(dims, dtype)


def merge(a, b):
    top = jnp.maximum(a, b)
    return top + jnp.log(jnp.exp(a - top) + jnp.exp(b - top))


def in_hbm(x):
    return pltpu.with_memory_space_constraint(x, pltpu.HBM)


def shards(tables, images, defocus, class_id, rotation_id, shift_id, references, owner, inv_noise, prior):
    cos, sin, turns, plain = [in_hbm(jnp.asarray(v)) for v in tables]
    mine = references[0]
    refs = lax.all_to_all(
        jnp.broadcast_to(mine[None], (BLKS,) + mine.shape).reshape(-1, FEAT), "blk", 0, 0, tiled=True
    )
    group = lax.axis_index("grp").astype(jnp.int32).reshape(1, 1)
    row = lambda v: in_hbm(v.reshape(1, -1))
    inv = row(inv_noise)
    owner = in_hbm(owner)
    images = in_hbm(images)
    what, y, crow, cexp, key, cp = pl.pallas_call(
        prep_kernel,
        grid=(KGRP,),
        in_specs=[
            pl.BlockSpec(memory_space=pltpu.SMEM),
            pl.BlockSpec((P_BLK, 128), lambda g: (0, g)),
            pl.BlockSpec((P_BLK, 128), lambda g: (0, g + KGRP)),
        ]
        + [whole((1, P_BLK))] * 4
        + [whole((1, C_GRP)), whole((1, CYCLES))]
        + [pl.BlockSpec((16, 128), lambda g: (0, g))] * 2
        + [pl.BlockSpec((128, 8), lambda g: (g, 0)), whole((512, 256))],
        out_specs=[
            pl.BlockSpec((SHIFTS, PAIRS, 1, 2, 16, P_BLK), lambda g: (0, 0, g, 0, 0, 0)),
            pl.BlockSpec((2, ROWS, 128), lambda g: (0, 0, g)),
            whole((ROWS, 128)),
            pl.BlockSpec((ROWS, 128), lambda g: (0, g)),
            whole((1, P_BLK)),
            whole((128, P_BLK)),
        ],
        out_shape=[
            pltpu.HBM((SHIFTS, PAIRS, KGRP, 2, 16, P_BLK), BF16),
            shape((2, ROWS, HALF)),
            shape((ROWS, 128)),
            shape((ROWS, HALF)),
            shape((1, P_BLK), jnp.int32),
            shape((128, P_BLK)),
        ],
        scratch_shapes=[
            pltpu.VMEM((ROWS, 128), F32),
            pltpu.VMEM((2, ROWS, 128), jnp.int32),
            pltpu.VMEM((KGRP, 8, P_BLK), F32),
        ],
        compiler_params=params(40),
        cost_estimate=pl.CostEstimate(flops=4 << 30, bytes_accessed=24 << 20, transcendentals=0),
        name="prep",
    )(
        group,
        images,
        images,
        row(defocus),
        row(class_id),
        row(rotation_id),
        row(shift_id),
        owner,
        inv,
        cos,
        sin,
        turns,
        plain,
    )
    what = in_hbm(what)
    lse, picked = pl.pallas_call(
        main_kernel,
        grid=(SHIFTS,),
        in_specs=[
            whole((C_GRP, FEAT)),
            pl.BlockSpec((1, PAIRS, KGRP, 2, 16, P_BLK), lambda t: (t, 0, 0, 0, 0, 0)),
            whole((512, 256)),
            whole((128, P_BLK)),
            whole((1, CYCLES)),
            whole((2, ROWS, HALF)),
            whole((ROWS, HALF)),
            whole((1, C_GRP)),
        ],
        out_specs=[whole((8, 128)), whole((ROWS, 128))],
        out_shape=[shape((8, 128)), shape((ROWS, 128))],
        scratch_shapes=[
            pltpu.VMEM((PAIRS, 256, 192), BF16),
            pltpu.VMEM((C_GRP, P_BLK), F32),
            pltpu.VMEM((PAIRS, 256, P_BLK), F32),
            pltpu.VMEM((8, P_BLK), F32),
            pltpu.VMEM((8, P_BLK), F32),
        ],
        compiler_params=params(40),
        name="score",
    )(refs, what, plain, cp, inv, y, cexp, owner)
    lse = merge(lse, lax.ppermute(lse, "grp", [(0, 1), (1, 0), (2, 3), (3, 2)]))
    lse = merge(lse, lax.ppermute(lse, "grp", [(0, 2), (2, 0), (1, 3), (3, 1)]))
    evidence = lse[:2].reshape(P_BLK) - LOG_ORIENTS
    partial = pl.pallas_call(
        weigh_kernel, out_shape=shape((C_GRP, WIDE)), compiler_params=params(16), name="weigh"
    )(lse, picked, key, y, crow)
    got = lax.all_to_all(partial, "blk", 0, 0, tiled=True)
    new_refs = pl.pallas_call(
        finish_kernel, out_shape=shape((CL_DEV, FEAT)), compiler_params=params(16), name="finish"
    )(got, row(prior))
    return (evidence, new_refs[None])


def solution(mesh):
    in_specs = (
        P("blk", None),
        P("blk"),
        P("blk", None),
        P("blk"),
        P("blk"),
        P("grp", "blk", None),
        P("grp", None),
        P(),
        P(),
    )
    out_specs = (P("blk"), P("grp", "blk", None))
    phase = phase_np().reshape(SHIFTS, HALF)
    pad = np.zeros((16 - SHIFTS, HALF))
    cos = np.concatenate([np.cos(phase), pad]).astype(np.float32)
    sin = np.concatenate([np.sin(phase), pad]).astype(np.float32)
    tables = (cos, sin, turn_table(), np.concatenate(split(dft_plain())))
    return jax.shard_map(
        functools.partial(shards, tables), mesh=mesh, in_specs=in_specs, out_specs=out_specs, check_vma=False
    )
```

```python
import functools
import math

import jax
import jax.numpy as jnp
import numpy as np
from jax import lax
from jax.experimental import pallas as pl
from jax.experimental.pallas import tpu as pltpu
from jax.sharding import PartitionSpec as P

CYCLES = 24
ANGLES = 32
SHIFTS = 9
CL_DEV = 2
P_BLK = 256
FEAT = 1536
HALF = FEAT // 2
C_GRP = 64
GROUPS = 4
CLASSES = 256
BLKS = 32
ROWS = 2 * C_GRP
PAIRS = 8
KGRP = 6
WIDE = FEAT + 128
LOG_ORIENTS = math.log(CLASSES * ANGLES * SHIFTS)
HIGH = lax.Precision.HIGHEST
F32 = jnp.float32
BF16 = jnp.bfloat16


def slot_place(s):
    if s == 0:
        return PAIRS - 1, 0
    if s == 8:
        return PAIRS - 1, 1
    return (s - 1, 0) if s < 8 else (15 - s, 1)


def phase_np():
    radius = (np.arange(CYCLES) + 1.0) / (2.0 * CYCLES)
    bearing = 2.0 * np.pi / ANGLES * np.arange(ANGLES)
    index = np.arange(SHIFTS)
    dx, dy = index // 3 - 1.0, index % 3 - 1.0
    along = dx[:, None] * np.cos(bearing) + dy[:, None] * np.sin(bearing)
    return -2.0 * np.pi * radius[None, :, None] * along[:, None, :]


def dft_rows():
    theta = 2.0 * np.pi / ANGLES
    angle = np.arange(ANGLES)
    out = np.zeros((16, 2, ANGLES))
    for s in range(1, 16):
        out[s, 0] = np.cos(theta * s * angle)
        out[s, 1] = -np.sin(theta * s * angle)
    out[0, 0] = 1.0
    out[0, 1] = np.cos(np.pi * angle)
    return out


def dft_plain():
    base = dft_rows()
    out = np.zeros((16, 2, 2, 4, 2, 4, ANGLES))
    for q in range(2):
        for k in range(4):
            out[:, :, q, k, q, k, :] = base
    return out.reshape(256, 256)


def turn_table():
    phase = phase_np().reshape(SHIFTS, HALF)
    px, py = phase[7], phase[5]
    columns = [np.cos(px), np.sin(px), np.cos(py), np.sin(py)]
    return np.stack(columns + columns, axis=1).astype(np.float32)


def phase_table():
    phase = phase_np().reshape(SHIFTS, HALF)
    rest = np.zeros((16, FEAT))
    rest[:SHIFTS] = np.concatenate([np.cos(phase), np.sin(phase)], axis=1)
    parts = []
    for _ in range(3):
        parts.append(rest.astype(np.float32).astype(jnp.bfloat16))
        rest = rest - parts[-1].astype(np.float64)
    return np.concatenate(parts)


def split(x):
    high = x.astype(np.float32).astype(jnp.bfloat16)
    low = (x - high.astype(np.float64)).astype(np.float32).astype(jnp.bfloat16)
    return high, low


def iota(shape, axis):
    return lax.broadcasted_iota(jnp.int32, shape, axis)


def as_column(row, n):
    same = iota((n, n), 0) == iota((n, n), 1)
    zero = jnp.zeros((), row.dtype)
    return jnp.sum(jnp.where(same, jnp.broadcast_to(row, (n, n)), zero), axis=1, keepdims=True)


def spread_cycles(row):
    column = as_column(row, CYCLES)
    hit = iota((CYCLES, HALF), 0) == iota((CYCLES, HALF), 1) // ANGLES
    return jnp.sum(jnp.where(hit, column, 0.0), axis=0, keepdims=True)


def parts_of(x):
    high = x.astype(BF16)
    rest = x - high.astype(F32)
    middle = rest.astype(BF16)
    return high, middle, (rest - middle.astype(F32)).astype(BF16)


def prep_kernel(group_ref, *refs):
    sources, refs = refs[:10], refs[10:]
    stored_ref, y_ref, crow_ref, cexp_ref, key_ref, cp_ref, where_ref, inv_ref, prior_ref, plain_ref, summing_ref = refs[:11]
    images_ref, defocus_ref, cls_ref, rot_ref, shf_ref, owner_ref, noise_ref, table_ref, turns_ref, sem = refs[11:21]
    raw_ref, what_ref, out_sem = refs[21:24]
    targets = (
        defocus_ref, cls_ref, rot_ref, shf_ref, owner_ref, noise_ref, raw_ref, images_ref, table_ref, turns_ref
    )
    copies = [pltpu.make_async_copy(sources[j], targets[j], sem.at[j]) for j in range(10)]
    copies.append(pltpu.make_async_copy(refs[24], plain_ref, sem.at[10]))
    copies.append(pltpu.make_async_copy(refs[25], summing_ref, sem.at[11]))
    for copy in copies:
        copy.start()
    for copy in copies[:7]:
        copy.wait()

    defocus, cls, owner = defocus_ref[...], cls_ref[...], owner_ref[...]
    frequency = (iota((CYCLES, 1), 0).astype(F32) + 1.0) / CYCLES
    contrast = -jnp.sin((frequency * frequency) * defocus + 0.15)
    noise = noise_ref[...]
    factor = contrast * as_column(noise, CYCLES)
    cp_ref[...] = contrast * factor
    inv_ref[...] = jnp.broadcast_to(spread_cycles(noise), (8, HALF))
    prior_ref[...] = jnp.zeros((8, 128), F32)
    prior_ref[:, :CYCLES] = jnp.broadcast_to(raw_ref[...], (8, CYCLES))

    local = cls - group_ref[0, 0] * C_GRP
    member = (local >= 0) & (local < C_GRP)
    cls_col = as_column(cls, P_BLK)
    earlier = (cls_col == cls) & (iota((P_BLK, P_BLK), 0) < iota((P_BLK, P_BLK), 1))
    turn = jnp.sum(jnp.where(earlier, 1, 0), axis=0, keepdims=True)
    owner_col = as_column(owner, C_GRP)
    hit = iota((C_GRP, P_BLK), 0) == local
    slot = jnp.sum(jnp.where(hit, owner_col, 0), axis=0, keepdims=True)
    key = jnp.where(member, turn * C_GRP + slot, -1)
    key_ref[...] = key
    where_ref[...] = (iota((C_GRP, C_GRP), 0) == owner).astype(F32)

    chosen = iota((ROWS, P_BLK), 0) == key
    pick = lambda row: jnp.sum(jnp.where(chosen, row, jnp.zeros((), row.dtype)), axis=1, keepdims=True)
    lane = iota((ROWS, 128), 1)
    freq = (lane[0:1].astype(F32) + 1.0) / CYCLES
    freq = jnp.where(freq <= 1.0, freq * freq, 0.0)
    crow = jnp.where(lane < CYCLES, -jnp.sin(pick(defocus) * freq + 0.15), 0.0)
    crow_ref[...] = crow
    expand = (iota((128, HALF), 0) == iota((128, HALF), 1) // ANGLES).astype(BF16)
    cexp = sum(jnp.dot(c, expand, preferred_element_type=F32) for c in parts_of(crow))
    cexp_ref[...] = cexp
    which = (iota((ROWS, 48), 1) % 16 == pick(shf_ref[...])).astype(BF16)
    source = (lane & ~(ANGLES - 1)) | ((lane + pick(rot_ref[...])) & (ANGLES - 1))
    for copy in copies[7:10]:
        copy.wait()
    phase = jnp.dot(which, table_ref[...], preferred_element_type=F32)
    gathered = jnp.dot(chosen.astype(BF16), images_ref[...], preferred_element_type=F32)
    for j in range(HALF // 128):
        lanes, others = slice(128 * j, 128 * (j + 1)), slice(HALF + 128 * j, HALF + 128 * (j + 1))
        cos, sin, real, imag = phase[:, lanes], phase[:, others], gathered[:, lanes], gathered[:, others]
        both = (cos * real + sin * imag, cos * imag - sin * real)
        for q in range(2):
            turned = jnp.take_along_axis(both[q], source, axis=1, mode="promise_in_bounds")
            y_ref[q, :, lanes] = turned * cexp[:, lanes]
    copies[10].wait()

    def moves(v0, v1, c, s):
        c0, c1, s0, s1 = c * v0, c * v1, s * v0, s * v1
        return [(c0 - s1, c1 + s0), (v0, v1), (c0 + s1, c1 - s0)]

    plain = plain_ref[:256]
    stores = []
    for g in range(KGRP):
        wide = jnp.concatenate(
            [jnp.broadcast_to(factor[4 * g + k : 4 * g + k + 1, :], (ANGLES, P_BLK)) for k in range(4)], axis=0
        )
        w0 = images_ref[:, 128 * g : 128 * (g + 1)].astype(F32).T * wide
        w1 = images_ref[:, HALF + 128 * g : HALF + 128 * (g + 1)].astype(F32).T * wide
        turns = turns_ref[128 * g : 128 * (g + 1), :]
        tables = [jnp.broadcast_to(turns[:, j : j + 1], (128, P_BLK)) for j in range(4)]
        for i, (a0, a1) in enumerate(moves(w0, w1, tables[0], tables[1])):
            for j, (b0, b1) in enumerate(moves(a0, a1, tables[2], tables[3])):
                x = jnp.concatenate([b0, b1], axis=0).astype(BF16)
                res = jnp.dot(plain, x, preferred_element_type=F32).astype(BF16)
                for s in range(16):
                    pair, side = slot_place(s)
                    what_ref[3 * i + j, pair, g, 16 * side : 16 * side + 16, :] = res[16 * s : 16 * s + 16]
            piece = slice(3 * i, 3 * i + 3)
            store = pltpu.make_async_copy(
                what_ref.at[piece, :, g], stored_ref.at[piece, :, g], out_sem.at[g, i]
            )
            store.start()
            stores.append(store)
    copies[11].wait()
    for store in stores:
        store.wait()


def real_idft4(e0, e2, re, im):
    a, b = e0 + e2, e0 - e2
    return [a + re, b + im, a - re, b - im]


def real_idft8(c0, c4, c1, c2, c3):
    r = math.sqrt(0.5)
    even = real_idft4(c0 + c4, c2[0], c1[0] + c3[0], c1[1] - c3[1])
    hr, hi = c1[0] - c3[0], c1[1] + c3[1]
    odd = real_idft4(c0 - c4, c2[1], (hr + hi) * r, (hi - hr) * r)
    return even + odd


def real_idft16(a0, a8, a):
    plus = {m: (a[m][0] + a[8 - m][0], a[m][1] - a[8 - m][1]) for m in (1, 2, 3)}
    even = real_idft8(a0 + a8, a[4][0], plus[1], plus[2], plus[3])
    turned = {}
    for m in (1, 2, 3):
        hr, hi = a[m][0] - a[8 - m][0], a[m][1] + a[8 - m][1]
        if m == 2:
            r = math.sqrt(0.5)
            turned[m] = ((hr + hi) * r, (hi - hr) * r)
        else:
            c, s = math.cos(2.0 * math.pi * m / 16), math.sin(2.0 * math.pi * m / 16)
            turned[m] = (hr * c + hi * s, hi * c - hr * s)
    odd = real_idft8(a0 - a8, a[4][1], turned[1], turned[2], turned[3])
    return even + odd


def fold(values, op):
    while len(values) > 1:
        values = [op(values[i], values[i + 1]) if i + 1 < len(values) else values[i] for i in range(0, len(values), 2)]
    return values[0]


def factors(refs, d_high, d_low, lhs_ref):
    scale = math.log2(math.e) / (ANGLES * math.sqrt(FEAT))
    pieces = []
    for h in range(3):
        halves = []
        for q in range(2):
            at = q * HALF + 256 * h
            both = jnp.concatenate([refs[:, at : at + 128], refs[:, at + 128 : at + 256]], axis=0)
            halves.append(both.T)
        pieces.append(jnp.concatenate(halves, axis=0))
    x = jnp.concatenate(pieces, axis=1)
    xh = x.astype(BF16)
    xl = (x - xh.astype(F32)).astype(BF16)
    res = jnp.dot(d_high, xh, preferred_element_type=F32)
    res = res + (jnp.dot(d_low, xh, preferred_element_type=F32) + jnp.dot(d_high, xl, preferred_element_type=F32))
    res = res * scale
    left = iota((8, 128), 1) < 64
    for pair in range(PAIRS):
        slots = (pair + 1, 15 - pair) if pair < PAIRS - 1 else (0, 8)
        blocks = [[[None] * 4 for _ in range(KGRP)] for _ in range(2)]
        for h in range(3):
            lanes = slice(128 * h, 128 * (h + 1))
            v = [(res[16 * s : 16 * s + 8, lanes], res[16 * s + 8 : 16 * s + 16, lanes]) for s in slots]
            outs = []
            if pair < PAIRS - 1:
                m = pair + 1
                c, s = 2.0 * math.cos(2.0 * math.pi * m / ANGLES), 2.0 * math.sin(2.0 * math.pi * m / ANGLES)
                (r0, i0), (r1, i1) = v
                outs.append(((2.0 * r0, 2.0 * i0), (2.0 * r1, 2.0 * i1)))
                outs.append(((2.0 * i0, -2.0 * r0), (-2.0 * i1, 2.0 * r1)))
                outs.append(((c * r0 + s * i0, c * i0 - s * r0), (s * i1 - c * r1, -c * i1 - s * r1)))
                outs.append(((c * i0 - s * r0, -c * r0 - s * i0), (c * i1 + s * r1, s * i1 - c * r1)))
            else:
                (r0, i0), (r1, i1) = v
                zero = jnp.zeros_like(r0)
                outs.append(((r0, i0), (zero, zero)))
                outs.append(((zero, zero), (2.0 * r1, 2.0 * i1)))
                outs.append(((r0, -i0), (zero, zero)))
                outs.append(((zero, zero), (2.0 * i1, -2.0 * r1)))
            for side in range(2):
                for part in range(2):
                    tiles = [o[side][part] for o in outs]
                    for two in range(2):
                        first, second = tiles[2 * two], tiles[2 * two + 1]
                        lower = jnp.where(left, first, pltpu.roll(second, 64, 1))
                        upper = jnp.where(left, pltpu.roll(first, 64, 1), second)
                        blocks[side][2 * h][2 * two + part] = lower
                        blocks[side][2 * h + 1][2 * two + part] = upper
        for two in range(2):
            tall = jnp.concatenate(
                [blocks[side][g][2 * two + part] for g in range(KGRP) for side in range(2) for part in range(2)], axis=0
            )
            lhs_ref[pair, 128 * two : 128 * (two + 1), :] = tall.T.astype(BF16)


def score_kernel(refs_ref, stored_ref, plain_ref, summing_ref, cp_ref, lse_ref, lhs_ref, pen_ref, even_ref, odd_ref, what_ref, sem):
    root = 1.0 / math.sqrt(FEAT)
    load = lambda t: pltpu.make_async_copy(stored_ref.at[t], what_ref.at[t], sem.at[t])
    for t in range(2):
        load(t).start()
    refs = refs_ref[...]
    factors(refs, plain_ref[:256], plain_ref[256:], lhs_ref)
    for t in range(2, SHIFTS):
        load(t).start()
    square = refs[:, :HALF] * refs[:, :HALF] + refs[:, HALF:] * refs[:, HALF:]
    power = jnp.dot(jnp.concatenate(parts_of(square), axis=0), summing_ref[...], preferred_element_type=F32)
    power = power[:C_GRP] + (power[C_GRP : 2 * C_GRP] + power[2 * C_GRP :])
    penalty = jnp.dot(power[:, :CYCLES], cp_ref[...], precision=HIGH, preferred_element_type=F32)
    pen_ref[...] = penalty * (0.5 * root * math.log2(math.e))

    def multiply(t, coef_ref):
        load(t).wait()
        for pair in range(PAIRS):
            right = what_ref[t, pair].reshape(192, P_BLK)
            coef_ref[pair] = jnp.dot(lhs_ref[pair], right, preferred_element_type=F32)

    def absorb(coef_ref, state):
        fresh_state = []
        for half in range(2):
            lanes = slice(128 * half, 128 * (half + 1))
            peak, total = state[half]
            for cb in range(C_GRP // 8):
                take = lambda pair, o: coef_ref[pair, 64 * o + 8 * cb : 64 * o + 8 * cb + 8, lanes]
                pen = pen_ref[8 * cb : 8 * cb + 8, lanes]
                out = []
                for o in (0, 2):
                    a = {m: (take(m - 1, o), take(m - 1, o + 1)) for m in range(1, 8)}
                    out += real_idft16(take(7, o) - pen, take(7, o + 1), a)
                fresh = jnp.maximum(peak, fold(out, jnp.maximum))
                total = total * jnp.exp2(peak - fresh) + fold([jnp.exp2(x - fresh) for x in out], jnp.add)
                peak = fresh
            fresh_state.append((peak, total))
        return fresh_state

    start = (jnp.full((8, 128), -1e30, F32), jnp.zeros((8, 128), F32))
    multiply(0, even_ref)

    def body(j, state):
        multiply(2 * j + 1, odd_ref)
        state = absorb(even_ref, state)
        multiply(2 * j + 2, even_ref)
        return absorb(odd_ref, state)

    state = lax.fori_loop(0, (SHIFTS - 1) // 2, body, [start, start])
    state = absorb(even_ref, state)
    rows = []
    for peak, total in state:
        top = jnp.max(peak, axis=0, keepdims=True)
        amount = jnp.sum(total * jnp.exp2(peak - top), axis=0, keepdims=True)
        rows.append(top * math.log(2.0) + jnp.log(amount))
    lse_ref[...] = jnp.concatenate(rows + [jnp.zeros((6, 128), F32)], axis=0)


def pick_kernel(refs_ref, y_ref, cexp_ref, where_ref, inv_ref, picked_ref):
    root = 1.0 / math.sqrt(FEAT)
    where = where_ref[...].astype(BF16)
    refs = refs_ref[...]
    placed = sum(jnp.dot(where, part, preferred_element_type=F32) for part in parts_of(refs))
    inv = inv_ref[0:1, :]
    for o in range(2):
        rows = slice(C_GRP * o, C_GRP * (o + 1))
        amount = jnp.zeros((C_GRP, HALF), F32)
        for q in range(2):
            v = placed[:, HALF * q : HALF * (q + 1)]
            scaled = cexp_ref[rows, :] * v
            amount = amount + (y_ref[q, rows, :] * v - 0.5 * scaled * scaled)
        picked_ref[rows, :] = jnp.broadcast_to(jnp.sum(amount * inv, axis=1, keepdims=True) * root, (C_GRP, 128))


def weigh_kernel(lse_ref, picked_ref, key_ref, y_ref, crow_ref, out_ref, evidence_ref):
    lse = jnp.concatenate([lse_ref[0:1, :], lse_ref[1:2, :]], axis=1)
    evidence_ref[...] = lse - LOG_ORIENTS
    chosen = iota((ROWS, P_BLK), 0) == key_ref[...]
    mine = jnp.sum(jnp.where(chosen, lse, 0.0), axis=1, keepdims=True)
    valid = jnp.sum(jnp.where(chosen, 1.0, 0.0), axis=1, keepdims=True) > 0.5
    weight = jnp.where(valid, jnp.exp(jnp.where(valid, picked_ref[:, 0:1] - mine + LOG_ORIENTS, 0.0)), 0.0)
    w0, w1 = weight[:C_GRP], weight[C_GRP:]

    def put(at, value):
        for j in range(BLKS):
            out_ref[j, :, at : at + 128] = value[2 * j : 2 * j + 2]

    for q in range(2):
        for j in range(HALF // 128):
            lanes = slice(128 * j, 128 * (j + 1))
            put(HALF * q + 128 * j, w0 * y_ref[q, :C_GRP, lanes] + w1 * y_ref[q, C_GRP:, lanes])
    c0, c1 = crow_ref[:C_GRP], crow_ref[C_GRP:]
    put(FEAT, w0 * c0 * c0 + w1 * c1 * c1)


def finish_kernel(got_ref, prior_ref, out_ref):
    total = fold([got_ref[j] for j in range(BLKS)], jnp.add)
    denom = jnp.concatenate([total[:, FEAT:] + prior_ref[0:2, :], jnp.ones((6, 128), F32)], axis=0)
    expand = (iota((128, HALF), 0) == iota((128, HALF), 1) // ANGLES).astype(BF16)
    wide = sum(jnp.dot(d, expand, preferred_element_type=F32) for d in parts_of(denom))[0:2]
    out_ref[:, :HALF] = total[:, :HALF] / wide
    out_ref[:, HALF:] = total[:, HALF:FEAT] / wide


def params(mib):
    return pltpu.CompilerParams(vmem_limit_bytes=mib << 20)


def whole(shape):
    return pl.BlockSpec(shape, lambda *_: (0,) * len(shape))


def shape(dims, dtype=F32):
    return jax.ShapeDtypeStruct(dims, dtype)


def merge(a, b):
    top = jnp.maximum(a, b)
    return top + jnp.log(jnp.exp(a - top) + jnp.exp(b - top))


def in_hbm(x):
    return pltpu.with_memory_space_constraint(x, pltpu.HBM)


def in_hbm(x):
    return pltpu.with_memory_space_constraint(x, pltpu.HBM)


def gather(mine):
    spread = jnp.broadcast_to(mine[None], (BLKS,) + mine.shape).reshape(-1, FEAT)
    return lax.all_to_all(spread, "blk", 0, 0, tiled=True)


def shards(tables, images, defocus, class_id, rotation_id, shift_id, references, owner, inv_noise, prior):
    table, turns, plain, summing = [in_hbm(jnp.asarray(v)) for v in tables]
    refs = gather(references[0])
    index = lambda name: lax.axis_index(name).astype(jnp.int32).reshape(1, 1)
    row = lambda v: in_hbm(v.reshape(1, -1))
    what, y, crow, cexp, key, cp, where, inv, prior, plain, summing = pl.pallas_call(
        lambda group, *refs: prep_kernel(group, *refs[:10], *refs[12:], *refs[10:12]),
        in_specs=[pl.BlockSpec(memory_space=pltpu.SMEM)] + [pl.BlockSpec(memory_space=pl.ANY)] * 12,
        out_specs=[pl.BlockSpec(memory_space=pltpu.HBM)] + [pl.BlockSpec(memory_space=pltpu.VMEM)] * 10,
        out_shape=[
            pltpu.HBM((SHIFTS, PAIRS, KGRP, 32, P_BLK), BF16),
            shape((2, ROWS, HALF)),
            shape((ROWS, 128)),
            shape((ROWS, HALF)),
            shape((1, P_BLK), jnp.int32),
            shape((CYCLES, P_BLK)),
            shape((C_GRP, C_GRP)),
            shape((8, HALF)),
            shape((8, 128)),
            shape((512, 256), BF16),
            shape((HALF, 128), BF16),
        ],
        scratch_shapes=[
            pltpu.VMEM((P_BLK, FEAT), BF16),
            pltpu.VMEM((1, P_BLK), F32),
            pltpu.VMEM((1, P_BLK), jnp.int32),
            pltpu.VMEM((1, P_BLK), jnp.int32),
            pltpu.VMEM((1, P_BLK), jnp.int32),
            pltpu.VMEM((1, C_GRP), jnp.int32),
            pltpu.VMEM((1, CYCLES), F32),
            pltpu.VMEM((48, FEAT), BF16),
            pltpu.VMEM((HALF, 8), F32),
            pltpu.SemaphoreType.DMA((12,)),
            pltpu.VMEM((1, CYCLES), F32),
            pltpu.VMEM((SHIFTS, PAIRS, KGRP, 32, P_BLK), BF16),
            pltpu.SemaphoreType.DMA((KGRP, 3)),
        ],
        compiler_params=params(24),
        cost_estimate=pl.CostEstimate(flops=4 << 30, bytes_accessed=9 << 20, transcendentals=0),
        name="prep",
    )(
        index("grp"),
        row(defocus),
        row(class_id),
        row(rotation_id),
        row(shift_id),
        in_hbm(owner),
        row(inv_noise),
        row(prior),
        in_hbm(images),
        table,
        turns,
        plain,
        summing,
    )
    lse = pl.pallas_call(
        score_kernel,
        in_specs=[
            pl.BlockSpec(memory_space=pltpu.VMEM),
            pl.BlockSpec(memory_space=pl.ANY),
            pl.BlockSpec(memory_space=pltpu.VMEM),
            pl.BlockSpec(memory_space=pltpu.VMEM),
            pl.BlockSpec(memory_space=pltpu.VMEM),
        ],
        out_shape=shape((8, 128)),
        scratch_shapes=[
            pltpu.VMEM((PAIRS, 256, 192), BF16),
            pltpu.VMEM((C_GRP, P_BLK), F32),
            pltpu.VMEM((PAIRS, 256, P_BLK), F32),
            pltpu.VMEM((PAIRS, 256, P_BLK), F32),
            pltpu.VMEM((SHIFTS, PAIRS, KGRP, 32, P_BLK), BF16),
            pltpu.SemaphoreType.DMA((SHIFTS,)),
        ],
        compiler_params=params(24),
        cost_estimate=pl.CostEstimate(flops=8 << 30, bytes_accessed=9 << 20, transcendentals=0),
        name="score",
    )(refs, in_hbm(what), plain, summing, cp)
    picked = pl.pallas_call(
        pick_kernel,
        out_shape=shape((ROWS, 128)),
        compiler_params=params(16),
        cost_estimate=pl.CostEstimate(flops=1 << 30, bytes_accessed=2 << 20, transcendentals=0),
        name="pick",
    )(refs, y, cexp, where, inv)
    lse = merge(lse, lax.ppermute(lse, "grp", [(0, 1), (1, 0), (2, 3), (3, 2)]))
    lse = merge(lse, lax.ppermute(lse, "grp", [(0, 2), (2, 0), (1, 3), (3, 1)]))
    partial, evidence = pl.pallas_call(
        weigh_kernel,
        out_shape=[shape((BLKS, CL_DEV, WIDE)), shape((1, P_BLK))],
        compiler_params=params(16),
        name="weigh",
    )(lse, picked, key, y, crow)
    got = lax.all_to_all(partial, "blk", 0, 0)
    new_refs = pl.pallas_call(
        finish_kernel, out_shape=shape((CL_DEV, FEAT)), compiler_params=params(16), name="finish"
    )(got, prior)
    return (evidence.reshape(P_BLK), new_refs[None])


def solution(mesh):
    in_specs = (
        P("blk", None),
        P("blk"),
        P("blk", None),
        P("blk"),
        P("blk"),
        P("grp", "blk", None),
        P("grp", None),
        P(),
        P(),
    )
    out_specs = (P("blk"), P("grp", "blk", None))
    summing = np.arange(HALF)[:, None] // ANGLES == np.arange(128)[None, :]
    tables = (phase_table(), turn_table(), np.concatenate(split(dft_plain())), summing.astype(jnp.bfloat16))
    return jax.shard_map(
        functools.partial(shards, tables), mesh=mesh, in_specs=in_specs, out_specs=out_specs, check_vma=False
    )
```

```python
import functools
import math

import jax
import jax.numpy as jnp
import numpy as np
from jax import lax
from jax.experimental import pallas as pl
from jax.experimental.pallas import tpu as pltpu
from jax.sharding import PartitionSpec as P

CYCLES = 24
ANGLES = 32
SHIFTS = 9
CL_DEV = 2
P_BLK = 256
FEAT = 1536
HALF = FEAT // 2
C_GRP = 64
GROUPS = 4
CLASSES = 256
BLKS = 32
ROWS = 2 * C_GRP
PAIRS = 8
KGRP = 6
WIDE = FEAT + 128
LOG_ORIENTS = math.log(CLASSES * ANGLES * SHIFTS)
HIGH = lax.Precision.HIGHEST
F32 = jnp.float32
BF16 = jnp.bfloat16


def slot_place(s):
    if s == 0:
        return PAIRS - 1, 0
    if s == 8:
        return PAIRS - 1, 1
    return (s - 1, 0) if s < 8 else (15 - s, 1)


def phase_np():
    radius = (np.arange(CYCLES) + 1.0) / (2.0 * CYCLES)
    bearing = 2.0 * np.pi / ANGLES * np.arange(ANGLES)
    index = np.arange(SHIFTS)
    dx, dy = index // 3 - 1.0, index % 3 - 1.0
    along = dx[:, None] * np.cos(bearing) + dy[:, None] * np.sin(bearing)
    return -2.0 * np.pi * radius[None, :, None] * along[:, None, :]


def dft_rows():
    theta = 2.0 * np.pi / ANGLES
    angle = np.arange(ANGLES)
    out = np.zeros((16, 2, ANGLES))
    for s in range(1, 16):
        out[s, 0] = np.cos(theta * s * angle)
        out[s, 1] = -np.sin(theta * s * angle)
    out[0, 0] = 1.0
    out[0, 1] = np.cos(np.pi * angle)
    return out


def dft_plain():
    base = dft_rows()
    out = np.zeros((16, 2, 2, 4, 2, 4, ANGLES))
    for q in range(2):
        for k in range(4):
            out[:, :, q, k, q, k, :] = base
    return out.reshape(256, 256)


def turn_table():
    phase = phase_np().reshape(SHIFTS, HALF)
    px, py = phase[7], phase[5]
    columns = [np.cos(px), np.sin(px), np.cos(py), np.sin(py)]
    return np.stack(columns + columns, axis=1).astype(np.float32)


def phase_table():
    phase = phase_np().reshape(SHIFTS, HALF)
    rest = np.zeros((16, FEAT))
    rest[:SHIFTS] = np.concatenate([np.cos(phase), np.sin(phase)], axis=1)
    parts = []
    for _ in range(3):
        parts.append(rest.astype(np.float32).astype(jnp.bfloat16))
        rest = rest - parts[-1].astype(np.float64)
    return np.concatenate(parts)


def split(x):
    high = x.astype(np.float32).astype(jnp.bfloat16)
    low = (x - high.astype(np.float64)).astype(np.float32).astype(jnp.bfloat16)
    return high, low


def iota(shape, axis):
    return lax.broadcasted_iota(jnp.int32, shape, axis)


def as_column(row, n):
    same = iota((n, n), 0) == iota((n, n), 1)
    zero = jnp.zeros((), row.dtype)
    return jnp.sum(jnp.where(same, jnp.broadcast_to(row, (n, n)), zero), axis=1, keepdims=True)


def spread_cycles(row):
    column = as_column(row, CYCLES)
    hit = iota((CYCLES, HALF), 0) == iota((CYCLES, HALF), 1) // ANGLES
    return jnp.sum(jnp.where(hit, column, 0.0), axis=0, keepdims=True)


def parts_of(x):
    high = x.astype(BF16)
    rest = x - high.astype(F32)
    middle = rest.astype(BF16)
    return high, middle, (rest - middle.astype(F32)).astype(BF16)


def prep_kernel(group_ref, *refs):
    sources, refs = refs[:10], refs[10:]
    stored_ref, y_ref, crow_ref, cexp_ref, key_ref, cp_ref, where_ref, inv_ref, prior_ref, plain_ref, summing_ref = refs[:11]
    images_ref, defocus_ref, cls_ref, rot_ref, shf_ref, owner_ref, noise_ref, table_ref, turns_ref, sem = refs[11:21]
    raw_ref, what_ref, out_sem = refs[21:24]
    targets = (
        defocus_ref, cls_ref, rot_ref, shf_ref, owner_ref, noise_ref, raw_ref, images_ref, table_ref, turns_ref
    )
    copies = [pltpu.make_async_copy(sources[j], targets[j], sem.at[j]) for j in range(10)]
    copies.append(pltpu.make_async_copy(refs[24], plain_ref, sem.at[10]))
    copies.append(pltpu.make_async_copy(refs[25], summing_ref, sem.at[11]))
    for copy in copies:
        copy.start()
    for copy in copies[:7]:
        copy.wait()

    defocus, cls, owner = defocus_ref[...], cls_ref[...], owner_ref[...]
    frequency = (iota((CYCLES, 1), 0).astype(F32) + 1.0) / CYCLES
    contrast = -jnp.sin((frequency * frequency) * defocus + 0.15)
    noise = noise_ref[...]
    factor = contrast * as_column(noise, CYCLES)
    cp_ref[...] = contrast * factor
    inv_ref[...] = jnp.broadcast_to(spread_cycles(noise), (8, HALF))
    prior_ref[...] = jnp.zeros((8, 128), F32)
    prior_ref[:, :CYCLES] = jnp.broadcast_to(raw_ref[...], (8, CYCLES))

    for j in (7, 9, 10):
        copies[j].wait()

    def moves(v0, v1, c, s):
        c0, c1, s0, s1 = c * v0, c * v1, s * v0, s * v1
        return [(c0 - s1, c1 + s0), (v0, v1), (c0 + s1, c1 - s0)]

    plain = plain_ref[:256]
    stores = []
    for g in range(KGRP):
        wide = jnp.concatenate(
            [jnp.broadcast_to(factor[4 * g + k : 4 * g + k + 1, :], (ANGLES, P_BLK)) for k in range(4)], axis=0
        )
        w0 = images_ref[:, 128 * g : 128 * (g + 1)].astype(F32).T * wide
        w1 = images_ref[:, HALF + 128 * g : HALF + 128 * (g + 1)].astype(F32).T * wide
        turns = turns_ref[128 * g : 128 * (g + 1), :]
        tables = [jnp.broadcast_to(turns[:, j : j + 1], (128, P_BLK)) for j in range(4)]
        for i, (a0, a1) in enumerate(moves(w0, w1, tables[0], tables[1])):
            for j, (b0, b1) in enumerate(moves(a0, a1, tables[2], tables[3])):
                x = jnp.concatenate([b0, b1], axis=0).astype(BF16)
                res = jnp.dot(plain, x, preferred_element_type=F32).astype(BF16)
                for s in range(16):
                    pair, side = slot_place(s)
                    what_ref[3 * i + j, pair, g, 16 * side : 16 * side + 16, :] = res[16 * s : 16 * s + 16]
            piece = slice(3 * i, 3 * i + 3)
            store = pltpu.make_async_copy(
                what_ref.at[piece, :, g], stored_ref.at[piece, :, g], out_sem.at[g, i]
            )
            store.start()
            stores.append(store)
    local = cls - group_ref[0, 0] * C_GRP
    member = (local >= 0) & (local < C_GRP)
    cls_col = as_column(cls, P_BLK)
    earlier = (cls_col == cls) & (iota((P_BLK, P_BLK), 0) < iota((P_BLK, P_BLK), 1))
    turn = jnp.sum(jnp.where(earlier, 1, 0), axis=0, keepdims=True)
    owner_col = as_column(owner, C_GRP)
    hit = iota((C_GRP, P_BLK), 0) == local
    slot = jnp.sum(jnp.where(hit, owner_col, 0), axis=0, keepdims=True)
    key = jnp.where(member, turn * C_GRP + slot, -1)
    key_ref[...] = key
    where_ref[...] = (iota((C_GRP, C_GRP), 0) == owner).astype(F32)

    chosen = iota((ROWS, P_BLK), 0) == key
    pick = lambda row: jnp.sum(jnp.where(chosen, row, jnp.zeros((), row.dtype)), axis=1, keepdims=True)
    lane = iota((ROWS, 128), 1)
    freq = (lane[0:1].astype(F32) + 1.0) / CYCLES
    freq = jnp.where(freq <= 1.0, freq * freq, 0.0)
    crow = jnp.where(lane < CYCLES, -jnp.sin(pick(defocus) * freq + 0.15), 0.0)
    crow_ref[...] = crow
    expand = (iota((128, HALF), 0) == iota((128, HALF), 1) // ANGLES).astype(BF16)
    cexp = sum(jnp.dot(c, expand, preferred_element_type=F32) for c in parts_of(crow))
    cexp_ref[...] = cexp
    which = (iota((ROWS, 48), 1) % 16 == pick(shf_ref[...])).astype(BF16)
    source = (lane & ~(ANGLES - 1)) | ((lane + pick(rot_ref[...])) & (ANGLES - 1))
    copies[8].wait()
    phase = jnp.dot(which, table_ref[...], preferred_element_type=F32)
    gathered = jnp.dot(chosen.astype(BF16), images_ref[...], preferred_element_type=F32)
    for j in range(HALF // 128):
        lanes, others = slice(128 * j, 128 * (j + 1)), slice(HALF + 128 * j, HALF + 128 * (j + 1))
        cos, sin, real, imag = phase[:, lanes], phase[:, others], gathered[:, lanes], gathered[:, others]
        both = (cos * real + sin * imag, cos * imag - sin * real)
        for q in range(2):
            turned = jnp.take_along_axis(both[q], source, axis=1, mode="promise_in_bounds")
            y_ref[q, :, lanes] = turned * cexp[:, lanes]
    copies[11].wait()
    for store in stores:
        store.wait()


def real_idft4(e0, e2, re, im):
    a, b = e0 + e2, e0 - e2
    return [a + re, b + im, a - re, b - im]


def real_idft8(c0, c4, c1, c2, c3):
    r = math.sqrt(0.5)
    even = real_idft4(c0 + c4, c2[0], c1[0] + c3[0], c1[1] - c3[1])
    hr, hi = c1[0] - c3[0], c1[1] + c3[1]
    odd = real_idft4(c0 - c4, c2[1], (hr + hi) * r, (hi - hr) * r)
    return even + odd


def real_idft16(a0, a8, a):
    plus = {m: (a[m][0] + a[8 - m][0], a[m][1] - a[8 - m][1]) for m in (1, 2, 3)}
    even = real_idft8(a0 + a8, a[4][0], plus[1], plus[2], plus[3])
    turned = {}
    for m in (1, 2, 3):
        hr, hi = a[m][0] - a[8 - m][0], a[m][1] + a[8 - m][1]
        if m == 2:
            r = math.sqrt(0.5)
            turned[m] = ((hr + hi) * r, (hi - hr) * r)
        else:
            c, s = math.cos(2.0 * math.pi * m / 16), math.sin(2.0 * math.pi * m / 16)
            turned[m] = (hr * c + hi * s, hi * c - hr * s)
    odd = real_idft8(a0 - a8, a[4][1], turned[1], turned[2], turned[3])
    return even + odd


def fold(values, op):
    while len(values) > 1:
        values = [op(values[i], values[i + 1]) if i + 1 < len(values) else values[i] for i in range(0, len(values), 2)]
    return values[0]


def factors(refs, d_high, d_low, lhs_ref):
    scale = math.log2(math.e) / (ANGLES * math.sqrt(FEAT))
    pieces = []
    for h in range(3):
        halves = []
        for q in range(2):
            at = q * HALF + 256 * h
            both = jnp.concatenate([refs[:, at : at + 128], refs[:, at + 128 : at + 256]], axis=0)
            halves.append(both.T)
        pieces.append(jnp.concatenate(halves, axis=0))
    x = jnp.concatenate(pieces, axis=1)
    xh = x.astype(BF16)
    xl = (x - xh.astype(F32)).astype(BF16)
    res = jnp.dot(d_high, xh, preferred_element_type=F32)
    res = res + (jnp.dot(d_low, xh, preferred_element_type=F32) + jnp.dot(d_high, xl, preferred_element_type=F32))
    res = res * scale
    left = iota((8, 128), 1) < 64
    for pair in range(PAIRS):
        slots = (pair + 1, 15 - pair) if pair < PAIRS - 1 else (0, 8)
        blocks = [[[None] * 4 for _ in range(KGRP)] for _ in range(2)]
        for h in range(3):
            lanes = slice(128 * h, 128 * (h + 1))
            v = [(res[16 * s : 16 * s + 8, lanes], res[16 * s + 8 : 16 * s + 16, lanes]) for s in slots]
            outs = []
            if pair < PAIRS - 1:
                m = pair + 1
                c, s = 2.0 * math.cos(2.0 * math.pi * m / ANGLES), 2.0 * math.sin(2.0 * math.pi * m / ANGLES)
                (r0, i0), (r1, i1) = v
                outs.append(((2.0 * r0, 2.0 * i0), (2.0 * r1, 2.0 * i1)))
                outs.append(((2.0 * i0, -2.0 * r0), (-2.0 * i1, 2.0 * r1)))
                outs.append(((c * r0 + s * i0, c * i0 - s * r0), (s * i1 - c * r1, -c * i1 - s * r1)))
                outs.append(((c * i0 - s * r0, -c * r0 - s * i0), (c * i1 + s * r1, s * i1 - c * r1)))
            else:
                (r0, i0), (r1, i1) = v
                zero = jnp.zeros_like(r0)
                outs.append(((r0, i0), (zero, zero)))
                outs.append(((zero, zero), (2.0 * r1, 2.0 * i1)))
                outs.append(((r0, -i0), (zero, zero)))
                outs.append(((zero, zero), (2.0 * i1, -2.0 * r1)))
            for side in range(2):
                for part in range(2):
                    tiles = [o[side][part] for o in outs]
                    for two in range(2):
                        first, second = tiles[2 * two], tiles[2 * two + 1]
                        lower = jnp.where(left, first, pltpu.roll(second, 64, 1))
                        upper = jnp.where(left, pltpu.roll(first, 64, 1), second)
                        blocks[side][2 * h][2 * two + part] = lower
                        blocks[side][2 * h + 1][2 * two + part] = upper
        for two in range(2):
            tall = jnp.concatenate(
                [blocks[side][g][2 * two + part] for g in range(KGRP) for side in range(2) for part in range(2)], axis=0
            )
            lhs_ref[pair, 128 * two : 128 * (two + 1), :] = tall.T.astype(BF16)


def score_kernel(refs_ref, stored_ref, plain_ref, summing_ref, cp_ref, lse_ref, lhs_ref, pen_ref, even_ref, odd_ref, what_ref, sem):
    root = 1.0 / math.sqrt(FEAT)
    load = lambda t: pltpu.make_async_copy(stored_ref.at[t], what_ref.at[t], sem.at[t])
    for t in range(2):
        load(t).start()
    refs = refs_ref[...]
    factors(refs, plain_ref[:256], plain_ref[256:], lhs_ref)
    for t in range(2, SHIFTS):
        load(t).start()
    square = refs[:, :HALF] * refs[:, :HALF] + refs[:, HALF:] * refs[:, HALF:]
    power = jnp.dot(jnp.concatenate(parts_of(square), axis=0), summing_ref[...], preferred_element_type=F32)
    power = power[:C_GRP] + (power[C_GRP : 2 * C_GRP] + power[2 * C_GRP :])
    penalty = jnp.dot(power[:, :CYCLES], cp_ref[...], precision=HIGH, preferred_element_type=F32)
    pen_ref[...] = penalty * (0.5 * root * math.log2(math.e))

    def multiply(t, coef_ref):
        load(t).wait()
        for pair in range(PAIRS):
            right = what_ref[t, pair].reshape(192, P_BLK)
            coef_ref[pair] = jnp.dot(lhs_ref[pair], right, preferred_element_type=F32)

    def absorb(coef_ref, state):
        fresh_state = []
        for half in range(2):
            lanes = slice(128 * half, 128 * (half + 1))
            peak, total = state[half]
            for cb in range(C_GRP // 8):
                take = lambda pair, o: coef_ref[pair, 64 * o + 8 * cb : 64 * o + 8 * cb + 8, lanes]
                pen = pen_ref[8 * cb : 8 * cb + 8, lanes]
                out = []
                for o in (0, 2):
                    a = {m: (take(m - 1, o), take(m - 1, o + 1)) for m in range(1, 8)}
                    out += real_idft16(take(7, o) - pen, take(7, o + 1), a)
                fresh = jnp.maximum(peak, fold(out, jnp.maximum))
                total = total * jnp.exp2(peak - fresh) + fold([jnp.exp2(x - fresh) for x in out], jnp.add)
                peak = fresh
            fresh_state.append((peak, total))
        return fresh_state

    start = (jnp.full((8, 128), -1e30, F32), jnp.zeros((8, 128), F32))
    multiply(0, even_ref)

    def body(j, state):
        multiply(2 * j + 1, odd_ref)
        state = absorb(even_ref, state)
        multiply(2 * j + 2, even_ref)
        return absorb(odd_ref, state)

    state = lax.fori_loop(0, (SHIFTS - 1) // 2, body, [start, start])
    state = absorb(even_ref, state)
    rows = []
    for peak, total in state:
        top = jnp.max(peak, axis=0, keepdims=True)
        amount = jnp.sum(total * jnp.exp2(peak - top), axis=0, keepdims=True)
        rows.append(top * math.log(2.0) + jnp.log(amount))
    lse_ref[...] = jnp.concatenate(rows + [jnp.zeros((6, 128), F32)], axis=0)


def pick_kernel(refs_ref, y_ref, cexp_ref, where_ref, inv_ref, picked_ref):
    root = 1.0 / math.sqrt(FEAT)
    where = where_ref[...].astype(BF16)
    refs = refs_ref[...]
    placed = sum(jnp.dot(where, part, preferred_element_type=F32) for part in parts_of(refs))
    inv = inv_ref[0:1, :]
    for o in range(2):
        rows = slice(C_GRP * o, C_GRP * (o + 1))
        amount = jnp.zeros((C_GRP, HALF), F32)
        for q in range(2):
            v = placed[:, HALF * q : HALF * (q + 1)]
            scaled = cexp_ref[rows, :] * v
            amount = amount + (y_ref[q, rows, :] * v - 0.5 * scaled * scaled)
        picked_ref[rows, :] = jnp.broadcast_to(jnp.sum(amount * inv, axis=1, keepdims=True) * root, (C_GRP, 128))


def weigh_kernel(lse_ref, picked_ref, key_ref, y_ref, crow_ref, out_ref):
    lse = jnp.concatenate([lse_ref[0:1, :], lse_ref[1:2, :]], axis=1)
    chosen = iota((ROWS, P_BLK), 0) == key_ref[...]
    mine = jnp.sum(jnp.where(chosen, lse, 0.0), axis=1, keepdims=True)
    valid = jnp.sum(jnp.where(chosen, 1.0, 0.0), axis=1, keepdims=True) > 0.5
    weight = jnp.where(valid, jnp.exp(jnp.where(valid, picked_ref[:, 0:1] - mine + LOG_ORIENTS, 0.0)), 0.0)
    w0, w1 = weight[:C_GRP], weight[C_GRP:]

    def put(at, value):
        for j in range(BLKS):
            out_ref[j, :, at : at + 128] = value[2 * j : 2 * j + 2]

    for q in range(2):
        for j in range(HALF // 128):
            lanes = slice(128 * j, 128 * (j + 1))
            put(HALF * q + 128 * j, w0 * y_ref[q, :C_GRP, lanes] + w1 * y_ref[q, C_GRP:, lanes])
    c0, c1 = crow_ref[:C_GRP], crow_ref[C_GRP:]
    put(FEAT, w0 * c0 * c0 + w1 * c1 * c1)


def finish_kernel(got_ref, prior_ref, lse_ref, out_ref, evidence_ref):
    evidence_ref[:, :128] = lse_ref[0:1, :] - LOG_ORIENTS
    evidence_ref[:, 128:] = lse_ref[1:2, :] - LOG_ORIENTS
    total = fold([got_ref[j] for j in range(BLKS)], jnp.add)
    denom = jnp.concatenate([total[:, FEAT:] + prior_ref[0:2, :], jnp.ones((6, 128), F32)], axis=0)
    expand = (iota((128, HALF), 0) == iota((128, HALF), 1) // ANGLES).astype(BF16)
    wide = sum(jnp.dot(d, expand, preferred_element_type=F32) for d in parts_of(denom))[0:2]
    out_ref[:, :HALF] = total[:, :HALF] / wide
    out_ref[:, HALF:] = total[:, HALF:FEAT] / wide


def params(mib):
    return pltpu.CompilerParams(vmem_limit_bytes=mib << 20)


def whole(shape):
    return pl.BlockSpec(shape, lambda *_: (0,) * len(shape))


def shape(dims, dtype=F32):
    return jax.ShapeDtypeStruct(dims, dtype)


def merge(a, b):
    top = jnp.maximum(a, b)
    return top + jnp.log(jnp.exp(a - top) + jnp.exp(b - top))


def in_hbm(x):
    return pltpu.with_memory_space_constraint(x, pltpu.HBM)


def in_hbm(x):
    return pltpu.with_memory_space_constraint(x, pltpu.HBM)


def gather(mine):
    spread = jnp.broadcast_to(mine[None], (BLKS,) + mine.shape).reshape(-1, FEAT)
    return lax.all_to_all(spread, "blk", 0, 0, tiled=True)


def shards(tables, images, defocus, class_id, rotation_id, shift_id, references, owner, inv_noise, prior):
    table, turns, plain, summing = [in_hbm(jnp.asarray(v)) for v in tables]
    refs = gather(references[0])
    index = lambda name: lax.axis_index(name).astype(jnp.int32).reshape(1, 1)
    row = lambda v: in_hbm(v.reshape(1, -1))
    what, y, crow, cexp, key, cp, where, inv, prior, plain, summing = pl.pallas_call(
        lambda group, *refs: prep_kernel(group, *refs[:10], *refs[12:], *refs[10:12]),
        in_specs=[pl.BlockSpec(memory_space=pltpu.SMEM)] + [pl.BlockSpec(memory_space=pl.ANY)] * 12,
        out_specs=[pl.BlockSpec(memory_space=pltpu.HBM)] + [pl.BlockSpec(memory_space=pltpu.VMEM)] * 10,
        out_shape=[
            pltpu.HBM((SHIFTS, PAIRS, KGRP, 32, P_BLK), BF16),
            shape((2, ROWS, HALF)),
            shape((ROWS, 128)),
            shape((ROWS, HALF)),
            shape((1, P_BLK), jnp.int32),
            shape((CYCLES, P_BLK)),
            shape((C_GRP, C_GRP)),
            shape((8, HALF)),
            shape((8, 128)),
            shape((512, 256), BF16),
            shape((HALF, 128), BF16),
        ],
        scratch_shapes=[
            pltpu.VMEM((P_BLK, FEAT), BF16),
            pltpu.VMEM((1, P_BLK), F32),
            pltpu.VMEM((1, P_BLK), jnp.int32),
            pltpu.VMEM((1, P_BLK), jnp.int32),
            pltpu.VMEM((1, P_BLK), jnp.int32),
            pltpu.VMEM((1, C_GRP), jnp.int32),
            pltpu.VMEM((1, CYCLES), F32),
            pltpu.VMEM((48, FEAT), BF16),
            pltpu.VMEM((HALF, 8), F32),
            pltpu.SemaphoreType.DMA((12,)),
            pltpu.VMEM((1, CYCLES), F32),
            pltpu.VMEM((SHIFTS, PAIRS, KGRP, 32, P_BLK), BF16),
            pltpu.SemaphoreType.DMA((KGRP, 3)),
        ],
        compiler_params=params(24),
        cost_estimate=pl.CostEstimate(flops=4 << 30, bytes_accessed=9 << 20, transcendentals=0),
        name="prep",
    )(
        index("grp"),
        row(defocus),
        row(class_id),
        row(rotation_id),
        row(shift_id),
        in_hbm(owner),
        row(inv_noise),
        row(prior),
        in_hbm(images),
        table,
        turns,
        plain,
        summing,
    )
    lse = pl.pallas_call(
        score_kernel,
        in_specs=[
            pl.BlockSpec(memory_space=pltpu.VMEM),
            pl.BlockSpec(memory_space=pl.ANY),
            pl.BlockSpec(memory_space=pltpu.VMEM),
            pl.BlockSpec(memory_space=pltpu.VMEM),
            pl.BlockSpec(memory_space=pltpu.VMEM),
        ],
        out_shape=shape((8, 128)),
        scratch_shapes=[
            pltpu.VMEM((PAIRS, 256, 192), BF16),
            pltpu.VMEM((C_GRP, P_BLK), F32),
            pltpu.VMEM((PAIRS, 256, P_BLK), F32),
            pltpu.VMEM((PAIRS, 256, P_BLK), F32),
            pltpu.VMEM((SHIFTS, PAIRS, KGRP, 32, P_BLK), BF16),
            pltpu.SemaphoreType.DMA((SHIFTS,)),
        ],
        compiler_params=params(24),
        cost_estimate=pl.CostEstimate(flops=8 << 30, bytes_accessed=9 << 20, transcendentals=0),
        name="score",
    )(refs, in_hbm(what), plain, summing, cp)
    picked = pl.pallas_call(
        pick_kernel,
        out_shape=shape((ROWS, 128)),
        compiler_params=params(16),
        cost_estimate=pl.CostEstimate(flops=1 << 30, bytes_accessed=2 << 20, transcendentals=0),
        name="pick",
    )(refs, y, cexp, where, inv)
    lse = merge(lse, lax.ppermute(lse, "grp", [(0, 1), (1, 0), (2, 3), (3, 2)]))
    lse = merge(lse, lax.ppermute(lse, "grp", [(0, 2), (2, 0), (1, 3), (3, 1)]))
    partial = pl.pallas_call(
        weigh_kernel,
        out_shape=shape((BLKS, CL_DEV, WIDE)),
        compiler_params=params(16),
        name="weigh",
    )(lse, picked, key, y, crow)
    got = lax.all_to_all(partial, "blk", 0, 0)
    new_refs, evidence = pl.pallas_call(
        finish_kernel,
        out_shape=[shape((CL_DEV, FEAT)), shape((1, P_BLK))],
        compiler_params=params(16),
        name="finish",
    )(got, prior, lse)
    return (evidence.reshape(P_BLK), new_refs[None])


def solution(mesh):
    in_specs = (
        P("blk", None),
        P("blk"),
        P("blk", None),
        P("blk"),
        P("blk"),
        P("grp", "blk", None),
        P("grp", None),
        P(),
        P(),
    )
    out_specs = (P("blk"), P("grp", "blk", None))
    summing = np.arange(HALF)[:, None] // ANGLES == np.arange(128)[None, :]
    tables = (phase_table(), turn_table(), np.concatenate(split(dft_plain())), summing.astype(jnp.bfloat16))
    return jax.shard_map(
        functools.partial(shards, tables), mesh=mesh, in_specs=in_specs, out_specs=out_specs, check_vma=False
    )
```

```python
import functools
import math

import jax
import jax.numpy as jnp
import numpy as np
from jax import lax
from jax.experimental import pallas as pl
from jax.experimental.pallas import tpu as pltpu
from jax.sharding import PartitionSpec as P

CYCLES = 24
ANGLES = 32
SHIFTS = 9
CL_DEV = 2
P_BLK = 256
FEAT = 1536
HALF = FEAT // 2
C_GRP = 64
GROUPS = 4
CLASSES = 256
BLKS = 32
ROWS = 2 * C_GRP
PAIRS = 8
KGRP = 6
WIDE = FEAT + 128
LOG_ORIENTS = math.log(CLASSES * ANGLES * SHIFTS)
HIGH = lax.Precision.HIGHEST
F32 = jnp.float32
BF16 = jnp.bfloat16


def slot_place(s):
    if s == 0:
        return PAIRS - 1, 0
    if s == 8:
        return PAIRS - 1, 1
    return (s - 1, 0) if s < 8 else (15 - s, 1)


def phase_np():
    radius = (np.arange(CYCLES) + 1.0) / (2.0 * CYCLES)
    bearing = 2.0 * np.pi / ANGLES * np.arange(ANGLES)
    index = np.arange(SHIFTS)
    dx, dy = index // 3 - 1.0, index % 3 - 1.0
    along = dx[:, None] * np.cos(bearing) + dy[:, None] * np.sin(bearing)
    return -2.0 * np.pi * radius[None, :, None] * along[:, None, :]


def dft_rows():
    theta = 2.0 * np.pi / ANGLES
    angle = np.arange(ANGLES)
    out = np.zeros((16, 2, ANGLES))
    for s in range(1, 16):
        out[s, 0] = np.cos(theta * s * angle)
        out[s, 1] = -np.sin(theta * s * angle)
    out[0, 0] = 1.0
    out[0, 1] = np.cos(np.pi * angle)
    return out


def dft_plain():
    base = dft_rows()
    out = np.zeros((16, 2, 2, 4, 2, 4, ANGLES))
    for q in range(2):
        for k in range(4):
            out[:, :, q, k, q, k, :] = base
    return out.reshape(256, 256)


def turn_table():
    phase = phase_np().reshape(SHIFTS, HALF)
    px, py = phase[7], phase[5]
    columns = [np.cos(px), np.sin(px), np.cos(py), np.sin(py)]
    return np.stack(columns + columns, axis=1).astype(np.float32)


def phase_table():
    phase = phase_np().reshape(SHIFTS, HALF)
    rest = np.zeros((16, FEAT))
    rest[:SHIFTS] = np.concatenate([np.cos(phase), np.sin(phase)], axis=1)
    parts = []
    for _ in range(3):
        parts.append(rest.astype(np.float32).astype(jnp.bfloat16))
        rest = rest - parts[-1].astype(np.float64)
    return np.concatenate(parts)


def split(x):
    high = x.astype(np.float32).astype(jnp.bfloat16)
    low = (x - high.astype(np.float64)).astype(np.float32).astype(jnp.bfloat16)
    return high, low


def iota(shape, axis):
    return lax.broadcasted_iota(jnp.int32, shape, axis)


def as_column(row, n):
    same = iota((n, n), 0) == iota((n, n), 1)
    zero = jnp.zeros((), row.dtype)
    return jnp.sum(jnp.where(same, jnp.broadcast_to(row, (n, n)), zero), axis=1, keepdims=True)


def spread_cycles(row):
    column = as_column(row, CYCLES)
    hit = iota((CYCLES, HALF), 0) == iota((CYCLES, HALF), 1) // ANGLES
    return jnp.sum(jnp.where(hit, column, 0.0), axis=0, keepdims=True)


def parts_of(x):
    high = x.astype(BF16)
    rest = x - high.astype(F32)
    middle = rest.astype(BF16)
    return high, middle, (rest - middle.astype(F32)).astype(BF16)


def prep_kernel(group_ref, *refs):
    sources, refs = refs[:10], refs[10:]
    stored_ref, y_ref, crow_ref, cexp_ref, key_ref, cp_ref, where_ref, inv_ref, prior_ref, plain_ref, summing_ref = refs[:11]
    images_ref, defocus_ref, cls_ref, rot_ref, shf_ref, owner_ref, noise_ref, table_ref, turns_ref, sem = refs[11:21]
    raw_ref, what_ref, out_sem = refs[21:24]
    targets = (
        defocus_ref, cls_ref, rot_ref, shf_ref, owner_ref, noise_ref, raw_ref, images_ref, table_ref, turns_ref
    )
    copies = [pltpu.make_async_copy(sources[j], targets[j], sem.at[j]) for j in range(10)]
    copies.append(pltpu.make_async_copy(refs[24], plain_ref, sem.at[10]))
    copies.append(pltpu.make_async_copy(refs[25], summing_ref, sem.at[11]))
    for copy in copies:
        copy.start()
    for copy in copies[:7]:
        copy.wait()

    defocus, cls, owner = defocus_ref[...], cls_ref[...], owner_ref[...]
    frequency = (iota((CYCLES, 1), 0).astype(F32) + 1.0) / CYCLES
    contrast = -jnp.sin((frequency * frequency) * defocus + 0.15)
    noise = noise_ref[...]
    factor = contrast * as_column(noise, CYCLES)
    cp_ref[...] = contrast * factor
    inv_ref[...] = jnp.broadcast_to(spread_cycles(noise), (8, HALF))
    prior_ref[...] = jnp.zeros((8, 128), F32)
    prior_ref[:, :CYCLES] = jnp.broadcast_to(raw_ref[...], (8, CYCLES))

    for j in (7, 9, 10):
        copies[j].wait()

    def moves(v0, v1, c, s):
        c0, c1, s0, s1 = c * v0, c * v1, s * v0, s * v1
        return [(c0 - s1, c1 + s0), (v0, v1), (c0 + s1, c1 - s0)]

    plain = plain_ref[:256]
    stores = []
    for g in range(KGRP):
        wide = jnp.concatenate(
            [jnp.broadcast_to(factor[4 * g + k : 4 * g + k + 1, :], (ANGLES, P_BLK)) for k in range(4)], axis=0
        )
        w0 = images_ref[:, 128 * g : 128 * (g + 1)].astype(F32).T * wide
        w1 = images_ref[:, HALF + 128 * g : HALF + 128 * (g + 1)].astype(F32).T * wide
        turns = turns_ref[128 * g : 128 * (g + 1), :]
        tables = [jnp.broadcast_to(turns[:, j : j + 1], (128, P_BLK)) for j in range(4)]
        for i, (a0, a1) in enumerate(moves(w0, w1, tables[0], tables[1])):
            for j, (b0, b1) in enumerate(moves(a0, a1, tables[2], tables[3])):
                x = jnp.concatenate([b0, b1], axis=0).astype(BF16)
                res = jnp.dot(plain, x, preferred_element_type=F32).astype(BF16)
                for s in range(16):
                    pair, side = slot_place(s)
                    what_ref[3 * i + j, pair, g, 16 * side : 16 * side + 16, :] = res[16 * s : 16 * s + 16]
            piece = slice(3 * i, 3 * i + 3)
            store = pltpu.make_async_copy(
                what_ref.at[piece, :, g], stored_ref.at[piece, :, g], out_sem.at[g, i]
            )
            store.start()
            stores.append(store)
    local = cls - group_ref[0, 0] * C_GRP
    member = (local >= 0) & (local < C_GRP)
    cls_col = as_column(cls, P_BLK)
    earlier = (cls_col == cls) & (iota((P_BLK, P_BLK), 0) < iota((P_BLK, P_BLK), 1))
    turn = jnp.sum(jnp.where(earlier, 1, 0), axis=0, keepdims=True)
    owner_col = as_column(owner, C_GRP)
    hit = iota((C_GRP, P_BLK), 0) == local
    slot = jnp.sum(jnp.where(hit, owner_col, 0), axis=0, keepdims=True)
    key = jnp.where(member, turn * C_GRP + slot, -1)
    key_ref[...] = key
    where_ref[...] = (iota((C_GRP, C_GRP), 0) == owner).astype(F32)

    chosen = iota((ROWS, P_BLK), 0) == key
    pick = lambda row: jnp.sum(jnp.where(chosen, row, jnp.zeros((), row.dtype)), axis=1, keepdims=True)
    lane = iota((ROWS, 128), 1)
    freq = (lane[0:1].astype(F32) + 1.0) / CYCLES
    freq = jnp.where(freq <= 1.0, freq * freq, 0.0)
    crow = jnp.where(lane < CYCLES, -jnp.sin(pick(defocus) * freq + 0.15), 0.0)
    crow_ref[...] = crow
    expand = (iota((128, HALF), 0) == iota((128, HALF), 1) // ANGLES).astype(BF16)
    cexp = sum(jnp.dot(c, expand, preferred_element_type=F32) for c in parts_of(crow))
    cexp_ref[...] = cexp
    which = (iota((ROWS, 48), 1) % 16 == pick(shf_ref[...])).astype(BF16)
    source = (lane & ~(ANGLES - 1)) | ((lane + pick(rot_ref[...])) & (ANGLES - 1))
    copies[8].wait()
    phase = jnp.dot(which, table_ref[...], preferred_element_type=F32)
    gathered = jnp.dot(chosen.astype(BF16), images_ref[...], preferred_element_type=F32)
    for j in range(HALF // 128):
        lanes, others = slice(128 * j, 128 * (j + 1)), slice(HALF + 128 * j, HALF + 128 * (j + 1))
        cos, sin, real, imag = phase[:, lanes], phase[:, others], gathered[:, lanes], gathered[:, others]
        both = (cos * real + sin * imag, cos * imag - sin * real)
        for q in range(2):
            turned = jnp.take_along_axis(both[q], source, axis=1, mode="promise_in_bounds")
            y_ref[q, :, lanes] = turned * cexp[:, lanes]
    copies[11].wait()
    for store in stores:
        store.wait()


def real_idft4(e0, e2, re, im):
    a, b = e0 + e2, e0 - e2
    return [a + re, b + im, a - re, b - im]


def real_idft8(c0, c4, c1, c2, c3, scale=1.0):
    r = scale * math.sqrt(0.5)
    re, im = c1[0] + c3[0], c1[1] - c3[1]
    if scale != 1.0:
        re, im = re * scale, im * scale
    even = real_idft4(c0 + c4, c2[0], re, im)
    hr, hi = c1[0] - c3[0], c1[1] + c3[1]
    odd = real_idft4(c0 - c4, c2[1], (hr + hi) * r, (hi - hr) * r)
    return even + odd


def real_idft16(a0, a8, a):
    plus = {m: (a[m][0] + a[8 - m][0], a[m][1] - a[8 - m][1]) for m in (1, 2, 3)}
    even = real_idft8(a0 + a8, a[4][0], plus[1], plus[2], plus[3])
    turned = {}
    for m in (1, 2, 3):
        hr, hi = a[m][0] - a[8 - m][0], a[m][1] + a[8 - m][1]
        if m == 2:
            r = math.sqrt(0.5)
            turned[m] = ((hr + hi) * r, (hi - hr) * r)
        else:
            t = math.tan(math.pi / 8)
            turned[m] = (hr + hi * t, hi - hr * t) if m == 1 else (hr * t + hi, hi * t - hr)
    odd = real_idft8(a0 - a8, a[4][1], turned[1], turned[2], turned[3], math.cos(math.pi / 8))
    return even + odd


def fold(values, op):
    while len(values) > 1:
        values = [op(values[i], values[i + 1]) if i + 1 < len(values) else values[i] for i in range(0, len(values), 2)]
    return values[0]


def factors(refs, d_high, d_low, lhs_ref):
    scale = math.log2(math.e) / (ANGLES * math.sqrt(FEAT))
    pieces = []
    for h in range(3):
        halves = []
        for q in range(2):
            at = q * HALF + 256 * h
            both = jnp.concatenate([refs[:, at : at + 128], refs[:, at + 128 : at + 256]], axis=0)
            halves.append(both.T)
        pieces.append(jnp.concatenate(halves, axis=0))
    x = jnp.concatenate(pieces, axis=1)
    xh = x.astype(BF16)
    xl = (x - xh.astype(F32)).astype(BF16)
    res = jnp.dot(d_high, xh, preferred_element_type=F32)
    res = res + (jnp.dot(d_low, xh, preferred_element_type=F32) + jnp.dot(d_high, xl, preferred_element_type=F32))
    res = res * scale
    left = iota((8, 128), 1) < 64
    for pair in range(PAIRS):
        slots = (pair + 1, 15 - pair) if pair < PAIRS - 1 else (0, 8)
        blocks = [[[None] * 4 for _ in range(KGRP)] for _ in range(2)]
        for h in range(3):
            lanes = slice(128 * h, 128 * (h + 1))
            v = [(res[16 * s : 16 * s + 8, lanes], res[16 * s + 8 : 16 * s + 16, lanes]) for s in slots]
            outs = []
            if pair < PAIRS - 1:
                m = pair + 1
                c, s = 2.0 * math.cos(2.0 * math.pi * m / ANGLES), 2.0 * math.sin(2.0 * math.pi * m / ANGLES)
                (r0, i0), (r1, i1) = v
                outs.append(((2.0 * r0, 2.0 * i0), (2.0 * r1, 2.0 * i1)))
                outs.append(((2.0 * i0, -2.0 * r0), (-2.0 * i1, 2.0 * r1)))
                outs.append(((c * r0 + s * i0, c * i0 - s * r0), (s * i1 - c * r1, -c * i1 - s * r1)))
                outs.append(((c * i0 - s * r0, -c * r0 - s * i0), (c * i1 + s * r1, s * i1 - c * r1)))
            else:
                (r0, i0), (r1, i1) = v
                zero = jnp.zeros_like(r0)
                outs.append(((r0, i0), (zero, zero)))
                outs.append(((zero, zero), (2.0 * r1, 2.0 * i1)))
                outs.append(((r0, -i0), (zero, zero)))
                outs.append(((zero, zero), (2.0 * i1, -2.0 * r1)))
            for side in range(2):
                for part in range(2):
                    tiles = [o[side][part] for o in outs]
                    for two in range(2):
                        first, second = tiles[2 * two], tiles[2 * two + 1]
                        lower = jnp.where(left, first, pltpu.roll(second, 64, 1))
                        upper = jnp.where(left, pltpu.roll(first, 64, 1), second)
                        blocks[side][2 * h][2 * two + part] = lower
                        blocks[side][2 * h + 1][2 * two + part] = upper
        for two in range(2):
            tall = jnp.concatenate(
                [blocks[side][g][2 * two + part] for g in range(KGRP) for side in range(2) for part in range(2)], axis=0
            )
            lhs_ref[pair, 128 * two : 128 * (two + 1), :] = tall.T.astype(BF16)


def score_kernel(refs_ref, stored_ref, plain_ref, summing_ref, cp_ref, lse_ref, lhs_ref, pen_ref, even_ref, odd_ref, what_ref, sem):
    root = 1.0 / math.sqrt(FEAT)
    load = lambda t: pltpu.make_async_copy(stored_ref.at[t], what_ref.at[t], sem.at[t])
    for t in range(2):
        load(t).start()
    refs = refs_ref[...]
    factors(refs, plain_ref[:256], plain_ref[256:], lhs_ref)
    for t in range(2, SHIFTS):
        load(t).start()
    square = refs[:, :HALF] * refs[:, :HALF] + refs[:, HALF:] * refs[:, HALF:]
    power = jnp.dot(jnp.concatenate(parts_of(square), axis=0), summing_ref[...], preferred_element_type=F32)
    power = power[:C_GRP] + (power[C_GRP : 2 * C_GRP] + power[2 * C_GRP :])
    penalty = jnp.dot(power[:, :CYCLES], cp_ref[...], precision=HIGH, preferred_element_type=F32)
    pen_ref[...] = penalty * (0.5 * root * math.log2(math.e))

    def multiply(t, coef_ref):
        load(t).wait()
        for pair in range(PAIRS):
            right = what_ref[t, pair].reshape(192, P_BLK)
            coef_ref[pair] = jnp.dot(lhs_ref[pair], right, preferred_element_type=F32)

    def absorb(coef_ref, state):
        fresh_state = []
        for half in range(2):
            lanes = slice(128 * half, 128 * (half + 1))
            peak, total = state[half]
            for cb in range(C_GRP // 8):
                take = lambda pair, o: coef_ref[pair, 64 * o + 8 * cb : 64 * o + 8 * cb + 8, lanes]
                pen = pen_ref[8 * cb : 8 * cb + 8, lanes]
                out = []
                for o in (0, 2):
                    a = {m: (take(m - 1, o), take(m - 1, o + 1)) for m in range(1, 8)}
                    out += real_idft16(take(7, o) - pen, take(7, o + 1), a)
                fresh = jnp.maximum(peak, fold(out, jnp.maximum))
                total = total * jnp.exp2(peak - fresh) + fold([jnp.exp2(x - fresh) for x in out], jnp.add)
                peak = fresh
            fresh_state.append((peak, total))
        return fresh_state

    start = (jnp.full((8, 128), -1e30, F32), jnp.zeros((8, 128), F32))
    multiply(0, even_ref)

    def body(j, state):
        multiply(2 * j + 1, odd_ref)
        state = absorb(even_ref, state)
        multiply(2 * j + 2, even_ref)
        return absorb(odd_ref, state)

    state = lax.fori_loop(0, (SHIFTS - 1) // 2, body, [start, start])
    state = absorb(even_ref, state)
    rows = []
    for peak, total in state:
        top = jnp.max(peak, axis=0, keepdims=True)
        amount = jnp.sum(total * jnp.exp2(peak - top), axis=0, keepdims=True)
        rows.append(top * math.log(2.0) + jnp.log(amount))
    lse_ref[...] = jnp.concatenate(rows + [jnp.zeros((6, 128), F32)], axis=0)


def pick_kernel(refs_ref, y_ref, cexp_ref, where_ref, inv_ref, picked_ref):
    root = 1.0 / math.sqrt(FEAT)
    where = where_ref[...].astype(BF16)
    refs = refs_ref[...]
    placed = sum(jnp.dot(where, part, preferred_element_type=F32) for part in parts_of(refs))
    inv = inv_ref[0:1, :]
    for o in range(2):
        rows = slice(C_GRP * o, C_GRP * (o + 1))
        amount = jnp.zeros((C_GRP, HALF), F32)
        for q in range(2):
            v = placed[:, HALF * q : HALF * (q + 1)]
            scaled = cexp_ref[rows, :] * v
            amount = amount + (y_ref[q, rows, :] * v - 0.5 * scaled * scaled)
        picked_ref[rows, :] = jnp.broadcast_to(jnp.sum(amount * inv, axis=1, keepdims=True) * root, (C_GRP, 128))


def weigh_kernel(lse_ref, picked_ref, key_ref, y_ref, crow_ref, out_ref):
    lse = jnp.concatenate([lse_ref[0:1, :], lse_ref[1:2, :]], axis=1)
    chosen = iota((ROWS, P_BLK), 0) == key_ref[...]
    mine = jnp.sum(jnp.where(chosen, lse, 0.0), axis=1, keepdims=True)
    valid = jnp.sum(jnp.where(chosen, 1.0, 0.0), axis=1, keepdims=True) > 0.5
    weight = jnp.where(valid, jnp.exp(jnp.where(valid, picked_ref[:, 0:1] - mine + LOG_ORIENTS, 0.0)), 0.0)
    w0, w1 = weight[:C_GRP], weight[C_GRP:]

    def put(at, value):
        for j in range(BLKS):
            out_ref[j, :, at : at + 128] = value[2 * j : 2 * j + 2]

    for q in range(2):
        for j in range(HALF // 128):
            lanes = slice(128 * j, 128 * (j + 1))
            put(HALF * q + 128 * j, w0 * y_ref[q, :C_GRP, lanes] + w1 * y_ref[q, C_GRP:, lanes])
    c0, c1 = crow_ref[:C_GRP], crow_ref[C_GRP:]
    put(FEAT, w0 * c0 * c0 + w1 * c1 * c1)


def finish_kernel(got_ref, prior_ref, lse_ref, out_ref, evidence_ref):
    evidence_ref[:, :128] = lse_ref[0:1, :] - LOG_ORIENTS
    evidence_ref[:, 128:] = lse_ref[1:2, :] - LOG_ORIENTS
    total = fold([got_ref[j] for j in range(BLKS)], jnp.add)
    denom = jnp.concatenate([total[:, FEAT:] + prior_ref[0:2, :], jnp.ones((6, 128), F32)], axis=0)
    expand = (iota((128, HALF), 0) == iota((128, HALF), 1) // ANGLES).astype(BF16)
    wide = sum(jnp.dot(d, expand, preferred_element_type=F32) for d in parts_of(denom))[0:2]
    out_ref[:, :HALF] = total[:, :HALF] / wide
    out_ref[:, HALF:] = total[:, HALF:FEAT] / wide


def params(mib):
    return pltpu.CompilerParams(vmem_limit_bytes=mib << 20)


def whole(shape):
    return pl.BlockSpec(shape, lambda *_: (0,) * len(shape))


def shape(dims, dtype=F32):
    return jax.ShapeDtypeStruct(dims, dtype)


def merge(a, b):
    top = jnp.maximum(a, b)
    return top + jnp.log(jnp.exp(a - top) + jnp.exp(b - top))


def in_hbm(x):
    return pltpu.with_memory_space_constraint(x, pltpu.HBM)


def in_hbm(x):
    return pltpu.with_memory_space_constraint(x, pltpu.HBM)


def gather(mine):
    spread = jnp.broadcast_to(mine[None], (BLKS,) + mine.shape).reshape(-1, FEAT)
    return lax.all_to_all(spread, "blk", 0, 0, tiled=True)


def shards(tables, images, defocus, class_id, rotation_id, shift_id, references, owner, inv_noise, prior):
    table, turns, plain, summing = [in_hbm(jnp.asarray(v)) for v in tables]
    refs = gather(references[0])
    index = lambda name: lax.axis_index(name).astype(jnp.int32).reshape(1, 1)
    row = lambda v: in_hbm(v.reshape(1, -1))
    what, y, crow, cexp, key, cp, where, inv, prior, plain, summing = pl.pallas_call(
        lambda group, *refs: prep_kernel(group, *refs[:10], *refs[12:], *refs[10:12]),
        in_specs=[pl.BlockSpec(memory_space=pltpu.SMEM)] + [pl.BlockSpec(memory_space=pl.ANY)] * 12,
        out_specs=[pl.BlockSpec(memory_space=pltpu.HBM)] + [pl.BlockSpec(memory_space=pltpu.VMEM)] * 10,
        out_shape=[
            pltpu.HBM((SHIFTS, PAIRS, KGRP, 32, P_BLK), BF16),
            shape((2, ROWS, HALF)),
            shape((ROWS, 128)),
            shape((ROWS, HALF)),
            shape((1, P_BLK), jnp.int32),
            shape((CYCLES, P_BLK)),
            shape((C_GRP, C_GRP)),
            shape((8, HALF)),
            shape((8, 128)),
            shape((512, 256), BF16),
            shape((HALF, 128), BF16),
        ],
        scratch_shapes=[
            pltpu.VMEM((P_BLK, FEAT), BF16),
            pltpu.VMEM((1, P_BLK), F32),
            pltpu.VMEM((1, P_BLK), jnp.int32),
            pltpu.VMEM((1, P_BLK), jnp.int32),
            pltpu.VMEM((1, P_BLK), jnp.int32),
            pltpu.VMEM((1, C_GRP), jnp.int32),
            pltpu.VMEM((1, CYCLES), F32),
            pltpu.VMEM((48, FEAT), BF16),
            pltpu.VMEM((HALF, 8), F32),
            pltpu.SemaphoreType.DMA((12,)),
            pltpu.VMEM((1, CYCLES), F32),
            pltpu.VMEM((SHIFTS, PAIRS, KGRP, 32, P_BLK), BF16),
            pltpu.SemaphoreType.DMA((KGRP, 3)),
        ],
        compiler_params=params(24),
        cost_estimate=pl.CostEstimate(flops=4 << 30, bytes_accessed=9 << 20, transcendentals=0),
        name="prep",
    )(
        index("grp"),
        row(defocus),
        row(class_id),
        row(rotation_id),
        row(shift_id),
        in_hbm(owner),
        row(inv_noise),
        row(prior),
        in_hbm(images),
        table,
        turns,
        plain,
        summing,
    )
    lse = pl.pallas_call(
        score_kernel,
        in_specs=[
            pl.BlockSpec(memory_space=pltpu.VMEM),
            pl.BlockSpec(memory_space=pl.ANY),
            pl.BlockSpec(memory_space=pltpu.VMEM),
            pl.BlockSpec(memory_space=pltpu.VMEM),
            pl.BlockSpec(memory_space=pltpu.VMEM),
        ],
        out_shape=shape((8, 128)),
        scratch_shapes=[
            pltpu.VMEM((PAIRS, 256, 192), BF16),
            pltpu.VMEM((C_GRP, P_BLK), F32),
            pltpu.VMEM((PAIRS, 256, P_BLK), F32),
            pltpu.VMEM((PAIRS, 256, P_BLK), F32),
            pltpu.VMEM((SHIFTS, PAIRS, KGRP, 32, P_BLK), BF16),
            pltpu.SemaphoreType.DMA((SHIFTS,)),
        ],
        compiler_params=params(24),
        cost_estimate=pl.CostEstimate(flops=8 << 30, bytes_accessed=9 << 20, transcendentals=0),
        name="score",
    )(refs, in_hbm(what), plain, summing, cp)
    picked = pl.pallas_call(
        pick_kernel,
        out_shape=shape((ROWS, 128)),
        compiler_params=params(16),
        cost_estimate=pl.CostEstimate(flops=1 << 30, bytes_accessed=2 << 20, transcendentals=0),
        name="pick",
    )(refs, y, cexp, where, inv)
    lse = merge(lse, lax.ppermute(lse, "grp", [(0, 1), (1, 0), (2, 3), (3, 2)]))
    lse = merge(lse, lax.ppermute(lse, "grp", [(0, 2), (2, 0), (1, 3), (3, 1)]))
    partial = pl.pallas_call(
        weigh_kernel,
        out_shape=shape((BLKS, CL_DEV, WIDE)),
        compiler_params=params(16),
        name="weigh",
    )(lse, picked, key, y, crow)
    got = lax.all_to_all(partial, "blk", 0, 0)
    new_refs, evidence = pl.pallas_call(
        finish_kernel,
        out_shape=[shape((CL_DEV, FEAT)), shape((1, P_BLK))],
        compiler_params=params(16),
        name="finish",
    )(got, prior, lse)
    return (evidence.reshape(P_BLK), new_refs[None])


def solution(mesh):
    in_specs = (
        P("blk", None),
        P("blk"),
        P("blk", None),
        P("blk"),
        P("blk"),
        P("grp", "blk", None),
        P("grp", None),
        P(),
        P(),
    )
    out_specs = (P("blk"), P("grp", "blk", None))
    summing = np.arange(HALF)[:, None] // ANGLES == np.arange(128)[None, :]
    tables = (phase_table(), turn_table(), np.concatenate(split(dft_plain())), summing.astype(jnp.bfloat16))
    return jax.shard_map(
        functools.partial(shards, tables), mesh=mesh, in_specs=in_specs, out_specs=out_specs, check_vma=False
    )
```
